128 devices in a mesh: dp: 16 (over x_hi, y, core), section: 8 (over x_lo, z).
Axes of the slice: x: 4 (x_hi: 2, x_lo: 2; x = x_hi * 2 + x_lo), y: 4, z: 4, core: 2. Of those that a mesh axis runs over, the one named last changes fastest.
Arguments:
- inputs: bfloat16 [2560, 8192], P('dp'), may hold values from -6 to 6
- cotangent: bfloat16 [2560, 8192], P('dp'), may hold values from -0.4375 to 0.4375
- weight_in: bfloat16 [8, 8192, 512], P('section'), may hold values from -0.0625 to 0.0625
- weight_out: bfloat16 [8, 8192, 512], P('section'), may hold values from -0.25 to 0.25
- norm_gains: float32 [8, 8192], P('section'), may hold values from 0.1 to 1.9
Outputs:
- in_grad: float32 [8, 8192, 512], P('section', 'dp')
- out_grad: float32 [8, 8192, 512], P('section', 'dp')
- gain_grad: float32 [8, 8192], P('section', 'dp')
The draws below stay inside these ranges and needn't reach their ends.
All inputs are finite; a program needn't handle non-finite values.
Results may differ from the reference program's by a relative error of at most 0.025.
Values may be sent and summed in bfloat16 or wider, within the bound.
No kernel may reach another device: no remote copies, remote signals or barrier semaphores. Data moves between devices by JAX's collectives and lax.ppermute only.
A program may use at most 192 MiB of HBM per device.

```python
import jax
import jax.numpy as jnp
from jax import lax

D = 8192
H = 512
SECTIONS = 8
TOK_DEV = 160
TOKENS = 2560
N_DP = 16


def raised(values, stream_key, source, target, shards_of, factor):
    owner, partner = [(jnp.arange(values.shape[position]) // (values.shape[position] // shards_of)).reshape([-1 if axis == position else 1 for axis in range(values.ndim)]) for position in (source, target)]
    chosen = jax.random.permutation(stream_key, shards_of)[partner]
    strong = (owner == chosen) | (owner == (partner + shards_of // 2) % shards_of)
    return jnp.where(strong, factor * values, values)


def shard_levels(stream_key, extent, cuts, low, top_value):
    loudness, own = 1.0, jax.random.fold_in(stream_key, 6)
    for dim, parts in cuts:
        heights = jnp.exp(jax.random.uniform(jax.random.fold_in(own, dim), (parts,), jnp.float32, low / len(cuts), top_value / len(cuts)))
        loudness = loudness * jnp.repeat(heights, extent[dim] // parts).reshape([-1 if axis == dim else 1 for axis in range(len(extent))])
    return loudness


def scatter_about(stream_key, dims, deviation, bound, shards=(), held_as=jnp.bfloat16):
    result = deviation * jax.random.normal(stream_key, dims, jnp.float32)
    if shards:
        result = result * shard_levels(stream_key, dims, shards, -0.22, 0.18)
    return jnp.clip(result, -bound, bound).astype(held_as)


def noise_with(key, shape, deviation, limit, shards, heavy, held_as=jnp.bfloat16):
    result = deviation * jax.random.normal(key, shape, jnp.float32)
    if shards:
        result = result * shard_levels(key, shape, shards, -0.22, 0.18)
    return jnp.clip(raised(result, jax.random.fold_in(key, 3), *heavy), -limit, limit).astype(held_as)


def setup_inputs(seed: int = 0) -> dict:
    key_of = jax.random.split(jax.random.key(seed), 6)
    inputs = scatter_about(key_of[0], (TOKENS, D), 1.0, 6.0, ((0, 16),))
    cotangent = noise_with(key_of[1], (TOKENS, D), (TOKENS ** -0.5), 0.4375, ((0, 16),), (0, 1, 16, 2.0))
    weight_in = scatter_about(key_of[2], (SECTIONS, D, H), D ** -0.5, 0.0625, ((0, 8),))
    weight_out = scatter_about(key_of[3], (SECTIONS, D, H), H ** -0.5, 0.25, ((0, 8),))
    norm_gains = jnp.clip(1.0 + 0.18 * jax.random.normal(key_of[4], (SECTIONS, D), jnp.float32), 0.1, 1.9)
    return {"inputs": inputs, "cotangent": cotangent, "weight_in": weight_in, "weight_out": weight_out, "norm_gains": norm_gains}


EPSILON = 1e-05

def normalize(block_rows, gain_row):
    values = block_rows.astype(jnp.float32)
    row_scale = lax.rsqrt(lax.optimization_barrier(jnp.mean(values * values, axis=1, keepdims=True)) + EPSILON)
    normed = (values * row_scale * gain_row).astype(jnp.bfloat16)
    return (values, row_scale, normed)

def layer_forward(block_rows, w_in, w_out, gain_row):
    values, row_scale, normed = normalize(block_rows, gain_row)
    pre_act = jnp.dot(normed, w_in, preferred_element_type=jnp.float32)
    activated = jax.nn.silu(pre_act).astype(jnp.bfloat16)
    branch = lax.dot_general(activated, w_out, (((1,), (1,)), ((), ())), preferred_element_type=jnp.float32)
    return (values + branch).astype(jnp.bfloat16)

def backward_parts(block_rows, upstream, w_in, w_out, gain_row):
    values, row_scale, normed = normalize(block_rows, gain_row)
    pre_act = jnp.dot(normed, w_in, preferred_element_type=jnp.float32)
    activated = jax.nn.silu(pre_act).astype(jnp.bfloat16)
    grad_act = jnp.dot(upstream, w_out, preferred_element_type=jnp.float32)
    sigmoid_pre = jax.nn.sigmoid(pre_act)
    grad_pre = (grad_act * sigmoid_pre * (1.0 + pre_act * (1.0 - sigmoid_pre))).astype(jnp.bfloat16)
    grad_norm = lax.dot_general(grad_pre, w_in, (((1,), (1,)), ((), ())), preferred_element_type=jnp.float32)
    scaled = grad_norm * gain_row
    centered = lax.optimization_barrier(jnp.mean(scaled * values, axis=1, keepdims=True))
    grad_in = (upstream.astype(jnp.float32) + row_scale * scaled - values * row_scale ** 3 * centered).astype(jnp.bfloat16)
    gain_rows = grad_norm * values * row_scale
    return (grad_in, normed, grad_pre, activated, gain_rows)

def column_product(left, right):
    return lax.dot_general(left, right, (((0,), (0,)), ((), ())), preferred_element_type=jnp.float32)

def reference(inputs, cotangent, weight_in, weight_out, norm_gains):
    hidden = [inputs]
    for section_id in range(SECTIONS - 1):
        hidden.append(layer_forward(hidden[-1], weight_in[section_id], weight_out[section_id], norm_gains[section_id]))
    upstream = cotangent
    in_list = [None] * SECTIONS
    out_list = [None] * SECTIONS
    gain_list = [None] * SECTIONS
    for section_id in reversed(range(SECTIONS)):
        grad_in, normed, grad_pre, activated, gain_rows = backward_parts(hidden[section_id], upstream, weight_in[section_id], weight_out[section_id], norm_gains[section_id])
        in_total = jnp.zeros((D, H), jnp.float32)
        out_total = jnp.zeros((D, H), jnp.float32)
        gain_total = jnp.zeros((D,), jnp.float32)
        for replica in range(N_DP):
            low = replica * TOK_DEV
            high = low + TOK_DEV
            in_term = column_product(normed[low:high], grad_pre[low:high])
            in_total = in_total + lax.optimization_barrier(in_term.astype(jnp.bfloat16)).astype(jnp.float32)
            out_term = column_product(upstream[low:high], activated[low:high])
            out_total = out_total + lax.optimization_barrier(out_term.astype(jnp.bfloat16)).astype(jnp.float32)
            gain_term = lax.optimization_barrier(jnp.sum(gain_rows[low:high], axis=0))
            gain_total = gain_total + lax.optimization_barrier(gain_term.astype(jnp.bfloat16)).astype(jnp.float32)
        in_list[section_id] = in_total
        out_list[section_id] = out_total
        gain_list[section_id] = gain_total
        upstream = grad_in
    return (jnp.stack(in_list), jnp.stack(out_list), jnp.stack(gain_list))
```

```python
import functools

import jax
import jax.numpy as jnp
from jax import lax
from jax.experimental import pallas as pl
from jax.experimental.pallas import tpu as pltpu
from jax.sharding import Mesh
from jax.sharding import PartitionSpec as P

ROWS = 16
CHUNK = 2048
SCOPED = 6 << 20
DP = ("dp_0", "dp_1", "dp_2")
CHIPS = ("dp_0", "dp_1")
CORE = "dp_2"
EPSILON = 1e-05

VMEM = pl.BlockSpec(memory_space=pltpu.VMEM)
SMEM = pl.BlockSpec(memory_space=pltpu.SMEM)
HBM = pl.BlockSpec(memory_space=pltpu.HBM)


def row_scale_of(rows_ref, width):
    def add(k, total):
        part = rows_ref[:, pl.ds(pl.multiple_of(k * CHUNK, CHUNK), CHUNK)].astype(jnp.float32)
        return total + jnp.sum(part * part, axis=1, keepdims=True)

    total = lax.fori_loop(0, width // CHUNK, add, jnp.zeros((ROWS, 1), jnp.float32))
    return lax.rsqrt(total / width + EPSILON)


def bring_in(tick, micro, first_at, ctl_ref, flag, came_ref, source_ref, rows_ref, sem):
    low = tick - first_at
    if not 0 <= low < micro:
        rows_ref[...] = came_ref[...]
        return
    mine = ctl_ref[flag] == 1

    @pl.when(mine)
    def _():
        fetch = pltpu.make_async_copy(source_ref.at[pl.ds(low * ROWS, ROWS), :], rows_ref, sem)
        fetch.start()
        fetch.wait()

    @pl.when(jnp.logical_not(mine))
    def _():
        rows_ref[...] = came_ref[...]


def forward_body(tick, micro, ctl_ref, came_ref, source_ref, w_in_far, w_out_far, gain_ref, *rest):
    (out_ref, rows_hbm, pre_hbm, w_in_ref, w_out_ref, rows_ref, pre_buf, source_sem, rows_sem, pre_sem, load_sem) = rest[-11:]
    width, hidden = w_in_ref.shape
    steps = width // CHUNK
    starting = tick == 0

    def load(which, k):
        far, near = ((w_in_far, w_in_ref), (w_out_far, w_out_ref))[which]
        cut = pl.ds(pl.multiple_of(k * CHUNK, CHUNK), CHUNK)
        return pltpu.make_async_copy(far.at[cut, :], near.at[cut, :], load_sem.at[which, k])

    if starting:
        for which in range(2):
            for k in range(steps):
                load(which, k).start()
    slot = ctl_ref[tick]
    flag = ctl_ref.shape[0] - 2
    bring_in(tick, micro, 0, ctl_ref, flag, came_ref, source_ref, rows_ref, source_sem)
    keep_rows = pltpu.make_async_copy(rows_ref, rows_hbm.at[slot], rows_sem)
    keep_rows.start()
    row_scale = row_scale_of(rows_ref, width)

    def project(k, pre):
        if starting:
            load(0, k).wait()
        cut = pl.ds(pl.multiple_of(k * CHUNK, CHUNK), CHUNK)
        normed = rows_ref[:, cut].astype(jnp.float32) * row_scale * gain_ref[:, cut]
        return pre + jnp.dot(
            normed.astype(jnp.bfloat16), w_in_ref[cut, :], preferred_element_type=jnp.float32
        )

    pre = lax.fori_loop(0, steps, project, jnp.zeros((ROWS, hidden), jnp.float32))
    pre_buf[:, :hidden] = pre
    pre_buf[:, hidden:] = jnp.broadcast_to(row_scale, (ROWS, 128))
    keep_pre = pltpu.make_async_copy(pre_buf, pre_hbm.at[slot], pre_sem)
    keep_pre.start()
    act = (pre * jax.nn.sigmoid(pre)).astype(jnp.bfloat16)

    def expand(k, carry):
        if starting:
            load(1, k).wait()
        cut = pl.ds(pl.multiple_of(k * CHUNK, CHUNK), CHUNK)
        branch = lax.dot_general(
            act, w_out_ref[cut, :], (((1,), (1,)), ((), ())), preferred_element_type=jnp.float32
        )
        out_ref[:, cut] = (rows_ref[:, cut].astype(jnp.float32) + branch).astype(jnp.bfloat16)
        return carry

    lax.fori_loop(0, steps, expand, 0)
    keep_rows.wait()
    keep_pre.wait()


def forward_step(tick, micro, ctl, came, source, w_in, w_out, gain, stores):
    width, hidden = w_in.shape
    count = 0 if stores is None else 2
    weight = VMEM if count else HBM
    same = {3: 3, 4: 4, 6: 1, 7: 2} if count else {}
    return pl.pallas_call(
        functools.partial(forward_body, tick, micro),
        out_shape=(
            jax.ShapeDtypeStruct((ROWS, width), jnp.bfloat16),
            jax.ShapeDtypeStruct((micro + 1, ROWS, width), jnp.bfloat16),
            jax.ShapeDtypeStruct((micro + 1, ROWS, hidden + 128), jnp.float32),
            pltpu.VMEM(w_in.shape, jnp.bfloat16),
            pltpu.VMEM(w_out.shape, jnp.bfloat16),
        ),
        in_specs=[SMEM, VMEM, HBM, weight, weight, VMEM] + [HBM] * count,
        out_specs=(VMEM, HBM, HBM, VMEM, VMEM),
        scratch_shapes=[
            pltpu.VMEM((ROWS, width), jnp.bfloat16),
            pltpu.VMEM((ROWS, hidden + 128), jnp.float32),
            pltpu.SemaphoreType.DMA,
            pltpu.SemaphoreType.DMA,
            pltpu.SemaphoreType.DMA,
            pltpu.SemaphoreType.DMA((2, width // CHUNK)),
        ],
        input_output_aliases=same,
        compiler_params=pltpu.CompilerParams(vmem_limit_bytes=SCOPED),
        name="forward_step",
    )(ctl, came, source, w_in, w_out, gain, *(stores or ()))


def backward_body(tick, micro, last, ctl_ref, came_ref, source_ref, w_in_ref, w_out_ref, gain_ref, *rest):
    (out_ref, rows_hbm, pre_hbm, up_hbm, pair_hbm, _, _, up_ref, rows_buf, pre_buf, pair_buf, sems) = rest[-12:]
    width, hidden = w_in_ref.shape
    steps = width // CHUNK
    slot = ctl_ref[micro + last + tick - last]
    flag = ctl_ref.shape[0] - 1
    get_pre = pltpu.make_async_copy(pre_hbm.at[slot], pre_buf, sems.at[1])
    get_pre.start()
    get_rows = pltpu.make_async_copy(rows_hbm.at[slot], rows_buf, sems.at[2])
    get_rows.start()
    bring_in(tick, micro, last, ctl_ref, flag, came_ref, source_ref, up_ref, sems.at[4])
    keep_up = pltpu.make_async_copy(up_ref, up_hbm.at[slot], sems.at[0])
    keep_up.start()

    def project(k, total):
        cut = pl.ds(pl.multiple_of(k * CHUNK, CHUNK), CHUNK)
        return total + jnp.dot(up_ref[:, cut], w_out_ref[cut, :], preferred_element_type=jnp.float32)

    grad_act = lax.fori_loop(0, steps, project, jnp.zeros((ROWS, hidden), jnp.float32))
    get_pre.wait()
    pre = pre_buf[:, :hidden]
    row_scale = pre_buf[:, hidden : hidden + 1]
    sig = jax.nn.sigmoid(pre)
    grad_pre = grad_act * sig * (1.0 + pre * (1.0 - sig))
    pair_buf[:, :hidden] = (grad_pre * row_scale).astype(jnp.bfloat16)
    pair_buf[:, hidden:] = (pre * sig).astype(jnp.bfloat16)
    keep_pair = pltpu.make_async_copy(pair_buf, pair_hbm.at[slot], sems.at[3])
    keep_pair.start()
    grad_cut = grad_pre.astype(jnp.bfloat16)
    pull = jnp.sum(grad_cut.astype(jnp.float32) * pre, axis=1, keepdims=True)
    pull = pull * row_scale * row_scale / width
    get_rows.wait()

    def expand(k, carry):
        cut = pl.ds(pl.multiple_of(k * CHUNK, CHUNK), CHUNK)
        grad_norm = lax.dot_general(
            grad_cut, w_in_ref[cut, :], (((1,), (1,)), ((), ())), preferred_element_type=jnp.float32
        )
        out_ref[:, cut] = (
            up_ref[:, cut].astype(jnp.float32)
            + row_scale * (grad_norm * gain_ref[:, cut])
            - rows_buf[:, cut].astype(jnp.float32) * pull
        ).astype(jnp.bfloat16)
        return carry

    lax.fori_loop(0, steps, expand, 0)
    keep_up.wait()
    keep_pair.wait()


def backward_step(tick, micro, last, ctl, came, source, w_in, w_out, gain, stores, kept):
    width, hidden = w_in.shape
    count = 0 if kept is None else 2
    return pl.pallas_call(
        functools.partial(backward_body, tick, micro, last),
        out_shape=(
            jax.ShapeDtypeStruct((ROWS, width), jnp.bfloat16),
            jax.ShapeDtypeStruct((micro + 1, ROWS, width), jnp.bfloat16),
            jax.ShapeDtypeStruct((micro + 1, ROWS, hidden + 128), jnp.float32),
            jax.ShapeDtypeStruct((micro + 1, ROWS, width), jnp.bfloat16),
            jax.ShapeDtypeStruct((micro + 1, ROWS, 2 * hidden), jnp.bfloat16),
            pltpu.VMEM(w_in.shape, jnp.bfloat16),
            pltpu.VMEM(w_out.shape, jnp.bfloat16),
        ),
        in_specs=[SMEM, VMEM, HBM, VMEM, VMEM, VMEM, HBM, HBM] + [HBM] * count,
        out_specs=(VMEM, HBM, HBM, HBM, HBM, VMEM, VMEM),
        scratch_shapes=[
            pltpu.VMEM((ROWS, width), jnp.bfloat16),
            pltpu.VMEM((ROWS, width), jnp.bfloat16),
            pltpu.VMEM((ROWS, hidden + 128), jnp.float32),
            pltpu.VMEM((ROWS, 2 * hidden), jnp.bfloat16),
            pltpu.SemaphoreType.DMA((5,)),
        ],
        input_output_aliases={3: 5, 4: 6, 6: 1, 7: 2, **{8 + k: 3 + k for k in range(count)}},
        compiler_params=pltpu.CompilerParams(vmem_limit_bytes=SCOPED),
        name="backward_step",
    )(ctl, came, source, w_in, w_out, gain, *stores, *(kept or ()))


def local(inputs, cotangent, weight_in, weight_out, norm_gains):
    w_in = weight_in[0]
    w_out = weight_out[0]
    gain = norm_gains
    tokens, width = inputs.shape
    hidden = w_in.shape[1]
    micro = tokens // ROWS
    sections = lax.axis_size("section")
    last = sections - 1
    pos = lax.axis_index("section")
    chips = lax.axis_size(CHIPS)
    onward = [(i, i + 1) for i in range(last)]
    back = [(i + 1, i) for i in range(last)]
    ticks = jnp.arange(micro + last)
    which = jnp.concatenate([ticks - pos, ticks - last + pos])
    slots = jnp.where((which >= 0) & (which < micro), which, micro)
    ends = jnp.stack([pos == 0, pos == last])
    ctl = jnp.concatenate([slots, ends]).astype(jnp.int32)
    ctl, w_in_near, w_out_near = lax.optimization_barrier((ctl, w_in, w_out))

    def spread(rows):
        tiles = rows.reshape(tokens, chips, -1).swapaxes(0, 1)
        return lax.all_to_all(tiles, CHIPS, split_axis=0, concat_axis=0, tiled=True)

    stores = None
    kept = None
    came = inputs[:ROWS]
    arriving = cotangent[:ROWS]
    rows_wide = None
    for tick in range(micro + 2 * last):
        if tick < micro + last:
            made, *stores, w_in_near, w_out_near = forward_step(
                tick, micro, ctl, came, inputs, w_in_near, w_out_near, gain, stores
            )
            came = lax.ppermute(made, "section", onward)
        if tick >= last:
            made, *both, w_in_near, w_out_near = backward_step(
                tick, micro, last, ctl, arriving, cotangent, w_in_near, w_out_near, gain, stores, kept
            )
            stores, kept = both[:2], both[2:]
            arriving = lax.ppermute(made, "section", back)
    rows_wide = spread(stores[0][:micro].reshape(tokens, width))
    up_wide = spread(kept[0][:micro].reshape(tokens, width)).reshape(chips * tokens, -1)
    pair = kept[1][:micro].reshape(1, tokens, 2 * hidden)
    pair_wide = lax.all_to_all(
        jnp.broadcast_to(pair, (chips, tokens, 2 * hidden)), CHIPS, split_axis=0, concat_axis=0, tiled=True
    ).reshape(chips * tokens, -1)
    rows_wide = rows_wide.reshape(chips * tokens, -1)

    def column_product(left, right):
        return lax.dot_general(
            left, right, (((0,), (0,)), ((), ())), preferred_element_type=jnp.float32
        )

    half = rows_wide.shape[1] // 2
    core = lax.axis_index(CORE)
    partial = jnp.concatenate(
        [column_product(rows_wide, pair_wide[:, :hidden]), column_product(up_wide, pair_wide[:, hidden:])],
        axis=1,
    )
    mine = lax.dynamic_slice_in_dim(partial, core * half, half, 0)
    theirs = lax.dynamic_slice_in_dim(partial, (1 - core) * half, half, 0).astype(jnp.bfloat16)
    total = mine + lax.ppermute(theirs, CORE, [(0, 1), (1, 0)]).astype(jnp.float32)
    plain = total[:, :hidden]
    low = lax.axis_index(DP) * half
    gain_cut = lax.dynamic_slice_in_dim(gain[0], low, half, 0)
    w_cut = lax.dynamic_slice_in_dim(w_in, low, half, 0).astype(jnp.float32)
    in_grad = plain * gain_cut[:, None]
    gain_grad = jnp.sum(plain * w_cut, axis=1)
    return (in_grad[None], total[None, :, hidden:], gain_grad[None])


def solution(mesh):
    finer = Mesh(
        mesh.devices.reshape(2, 4, 2, mesh.shape["section"]), ("dp_0", "dp_1", "dp_2", "section")
    )
    in_specs = (
        P(DP, None),
        P(DP, None),
        P("section", None, None),
        P("section", None, None),
        P("section", None),
    )
    out_specs = (P("section", DP, None), P("section", DP, None), P("section", DP))
    return jax.shard_map(local, mesh=finer, in_specs=in_specs, out_specs=out_specs, check_vma=False)
```

```python
import functools

import jax
import jax.numpy as jnp
from jax import lax
from jax.experimental import pallas as pl
from jax.experimental.pallas import tpu as pltpu
from jax.sharding import Mesh
from jax.sharding import PartitionSpec as P

ROWS = 16
CHUNK = 2048
SCOPED = 6 << 20
DP = ("dp_0", "dp_1", "dp_2")
CHIPS = ("dp_0", "dp_1")
CORE = "dp_2"
EPSILON = 1e-05

VMEM = pl.BlockSpec(memory_space=pltpu.VMEM)
SMEM = pl.BlockSpec(memory_space=pltpu.SMEM)
HBM = pl.BlockSpec(memory_space=pltpu.HBM)


def row_scale_of(rows_ref, width):
    def add(k, total):
        part = rows_ref[:, pl.ds(pl.multiple_of(k * CHUNK, CHUNK), CHUNK)].astype(jnp.float32)
        return total + jnp.sum(part * part, axis=1, keepdims=True)

    total = lax.fori_loop(0, width // CHUNK, add, jnp.zeros((ROWS, 1), jnp.float32))
    return lax.rsqrt(total / width + EPSILON)


def bring_in(tick, micro, first_at, ctl_ref, flag, came_ref, source_ref, rows_ref, sem):
    low = tick - first_at
    if not 0 <= low < micro:
        rows_ref[...] = came_ref[...]
        return
    mine = ctl_ref[flag] == 1

    @pl.when(mine)
    def _():
        fetch = pltpu.make_async_copy(source_ref.at[pl.ds(low * ROWS, ROWS), :], rows_ref, sem)
        fetch.start()
        fetch.wait()

    @pl.when(jnp.logical_not(mine))
    def _():
        rows_ref[...] = came_ref[...]


def forward_body(tick, micro, ctl_ref, came_ref, source_ref, w_in_far, w_out_far, gain_ref, *rest):
    (out_ref, rows_hbm, pre_hbm, w_in_ref, w_out_ref, rows_ref, pre_buf, source_sem, rows_sem, pre_sem, load_sem) = rest[-11:]
    width, hidden = w_in_ref.shape
    steps = width // CHUNK
    starting = tick == 0

    def load(which, k):
        far, near = ((w_in_far, w_in_ref), (w_out_far, w_out_ref))[which]
        cut = pl.ds(pl.multiple_of(k * CHUNK, CHUNK), CHUNK)
        return pltpu.make_async_copy(far.at[cut, :], near.at[cut, :], load_sem.at[which, k])

    if starting:
        for which in range(2):
            for k in range(steps):
                load(which, k).start()
    slot = ctl_ref[tick]
    flag = ctl_ref.shape[0] - 2
    bring_in(tick, micro, 0, ctl_ref, flag, came_ref, source_ref, rows_ref, source_sem)
    keep_rows = pltpu.make_async_copy(rows_ref, rows_hbm.at[slot], rows_sem)
    keep_rows.start()
    row_scale = row_scale_of(rows_ref, width)

    def project(k, pre):
        if starting:
            load(0, k).wait()
        cut = pl.ds(pl.multiple_of(k * CHUNK, CHUNK), CHUNK)
        normed = rows_ref[:, cut].astype(jnp.float32) * row_scale * gain_ref[:, cut]
        return pre + jnp.dot(
            normed.astype(jnp.bfloat16), w_in_ref[cut, :], preferred_element_type=jnp.float32
        )

    pre = lax.fori_loop(0, steps, project, jnp.zeros((ROWS, hidden), jnp.float32))
    pre_buf[:, :hidden] = pre
    pre_buf[:, hidden:] = jnp.broadcast_to(row_scale, (ROWS, 128))
    keep_pre = pltpu.make_async_copy(pre_buf, pre_hbm.at[slot], pre_sem)
    keep_pre.start()
    act = (pre * jax.nn.sigmoid(pre)).astype(jnp.bfloat16)

    def expand(k, carry):
        if starting:
            load(1, k).wait()
        cut = pl.ds(pl.multiple_of(k * CHUNK, CHUNK), CHUNK)
        branch = lax.dot_general(
            act, w_out_ref[cut, :], (((1,), (1,)), ((), ())), preferred_element_type=jnp.float32
        )
        out_ref[:, cut] = (rows_ref[:, cut].astype(jnp.float32) + branch).astype(jnp.bfloat16)
        return carry

    lax.fori_loop(0, steps, expand, 0)
    keep_rows.wait()
    keep_pre.wait()


def forward_step(tick, micro, ctl, came, source, w_in, w_out, gain, stores):
    width, hidden = w_in.shape
    count = 0 if stores is None else 2
    weight = VMEM if count else HBM
    same = {3: 3, 4: 4, 6: 1, 7: 2} if count else {}
    return pl.pallas_call(
        functools.partial(forward_body, tick, micro),
        out_shape=(
            jax.ShapeDtypeStruct((ROWS, width), jnp.bfloat16),
            jax.ShapeDtypeStruct((micro + 1, ROWS, width), jnp.bfloat16),
            jax.ShapeDtypeStruct((micro + 1, ROWS, hidden + 128), jnp.float32),
            pltpu.VMEM(w_in.shape, jnp.bfloat16),
            pltpu.VMEM(w_out.shape, jnp.bfloat16),
        ),
        in_specs=[SMEM, VMEM, HBM, weight, weight, VMEM] + [HBM] * count,
        out_specs=(VMEM, HBM, HBM, VMEM, VMEM),
        scratch_shapes=[
            pltpu.VMEM((ROWS, width), jnp.bfloat16),
            pltpu.VMEM((ROWS, hidden + 128), jnp.float32),
            pltpu.SemaphoreType.DMA,
            pltpu.SemaphoreType.DMA,
            pltpu.SemaphoreType.DMA,
            pltpu.SemaphoreType.DMA((2, width // CHUNK)),
        ],
        input_output_aliases=same,
        compiler_params=pltpu.CompilerParams(vmem_limit_bytes=SCOPED),
        name="forward_step",
    )(ctl, came, source, w_in, w_out, gain, *(stores or ()))


def backward_body(tick, micro, last, ctl_ref, came_ref, source_ref, w_in_ref, w_out_ref, gain_ref, *rest):
    (out_ref, rows_hbm, pre_hbm, up_hbm, pair_hbm, _, _, up_ref, rows_buf, pre_buf, pair_buf, sems) = rest[-12:]
    width, hidden = w_in_ref.shape
    steps = width // CHUNK
    slot = ctl_ref[micro + last + tick - last]
    flag = ctl_ref.shape[0] - 1
    get_pre = pltpu.make_async_copy(pre_hbm.at[slot], pre_buf, sems.at[1])
    get_pre.start()
    get_rows = pltpu.make_async_copy(rows_hbm.at[slot], rows_buf, sems.at[2])
    get_rows.start()
    bring_in(tick, micro, last, ctl_ref, flag, came_ref, source_ref, up_ref, sems.at[4])
    keep_up = pltpu.make_async_copy(up_ref, up_hbm.at[slot], sems.at[0])
    keep_up.start()

    def project(k, total):
        cut = pl.ds(pl.multiple_of(k * CHUNK, CHUNK), CHUNK)
        return total + jnp.dot(up_ref[:, cut], w_out_ref[cut, :], preferred_element_type=jnp.float32)

    grad_act = lax.fori_loop(0, steps, project, jnp.zeros((ROWS, hidden), jnp.float32))
    get_pre.wait()
    pre = pre_buf[:, :hidden]
    row_scale = pre_buf[:, hidden : hidden + 1]
    sig = jax.nn.sigmoid(pre)
    grad_pre = grad_act * sig * (1.0 + pre * (1.0 - sig))
    pair_buf[:, :hidden] = (grad_pre * row_scale).astype(jnp.bfloat16)
    pair_buf[:, hidden:] = (pre * sig).astype(jnp.bfloat16)
    keep_pair = pltpu.make_async_copy(pair_buf, pair_hbm.at[slot], sems.at[3])
    keep_pair.start()
    grad_cut = grad_pre.astype(jnp.bfloat16)
    pull = jnp.sum(grad_cut.astype(jnp.float32) * pre, axis=1, keepdims=True)
    pull = pull * row_scale * row_scale / width
    get_rows.wait()

    def expand(k, carry):
        cut = pl.ds(pl.multiple_of(k * CHUNK, CHUNK), CHUNK)
        grad_norm = lax.dot_general(
            grad_cut, w_in_ref[cut, :], (((1,), (1,)), ((), ())), preferred_element_type=jnp.float32
        )
        out_ref[:, cut] = (
            up_ref[:, cut].astype(jnp.float32)
            + row_scale * (grad_norm * gain_ref[:, cut])
            - rows_buf[:, cut].astype(jnp.float32) * pull
        ).astype(jnp.bfloat16)
        return carry

    lax.fori_loop(0, steps, expand, 0)
    keep_up.wait()
    keep_pair.wait()


def backward_step(tick, micro, last, ctl, came, source, w_in, w_out, gain, stores, kept):
    width, hidden = w_in.shape
    count = 0 if kept is None else 2
    return pl.pallas_call(
        functools.partial(backward_body, tick, micro, last),
        out_shape=(
            jax.ShapeDtypeStruct((ROWS, width), jnp.bfloat16),
            jax.ShapeDtypeStruct((micro + 1, ROWS, width), jnp.bfloat16),
            jax.ShapeDtypeStruct((micro + 1, ROWS, hidden + 128), jnp.float32),
            jax.ShapeDtypeStruct((micro + 1, ROWS, width), jnp.bfloat16),
            jax.ShapeDtypeStruct((micro + 1, ROWS, 2 * hidden), jnp.bfloat16),
            pltpu.VMEM(w_in.shape, jnp.bfloat16),
            pltpu.VMEM(w_out.shape, jnp.bfloat16),
        ),
        in_specs=[SMEM, VMEM, HBM, VMEM, VMEM, VMEM, HBM, HBM] + [HBM] * count,
        out_specs=(VMEM, HBM, HBM, HBM, HBM, VMEM, VMEM),
        scratch_shapes=[
            pltpu.VMEM((ROWS, width), jnp.bfloat16),
            pltpu.VMEM((ROWS, width), jnp.bfloat16),
            pltpu.VMEM((ROWS, hidden + 128), jnp.float32),
            pltpu.VMEM((ROWS, 2 * hidden), jnp.bfloat16),
            pltpu.SemaphoreType.DMA((5,)),
        ],
        input_output_aliases={3: 5, 4: 6, 6: 1, 7: 2, **{8 + k: 3 + k for k in range(count)}},
        compiler_params=pltpu.CompilerParams(vmem_limit_bytes=SCOPED),
        name="backward_step",
    )(ctl, came, source, w_in, w_out, gain, *stores, *(kept or ()))


def local(inputs, cotangent, weight_in, weight_out, norm_gains):
    w_in = weight_in[0]
    w_out = weight_out[0]
    gain = norm_gains
    tokens, width = inputs.shape
    hidden = w_in.shape[1]
    micro = tokens // ROWS
    sections = lax.axis_size("section")
    last = sections - 1
    pos = lax.axis_index("section")
    chips = lax.axis_size(CHIPS)
    onward = [(i, (i + 1) % sections) for i in range(sections)]
    back = [((i + 1) % sections, i) for i in range(sections)]
    ticks = jnp.arange(micro + last)
    which = jnp.concatenate([ticks - pos, ticks - last + pos])
    slots = jnp.where((which >= 0) & (which < micro), which, micro)
    ends = jnp.stack([pos == 0, pos == last])
    ctl = jnp.concatenate([slots, ends]).astype(jnp.int32)
    ctl, w_in_near, w_out_near = lax.optimization_barrier((ctl, w_in, w_out))

    def spread(rows):
        tiles = rows.reshape(tokens, chips, -1).swapaxes(0, 1)
        return lax.all_to_all(tiles, CHIPS, split_axis=0, concat_axis=0, tiled=True)

    stores = None
    kept = None
    came = inputs[:ROWS]
    arriving = cotangent[:ROWS]
    rows_wide = None
    for tick in range(micro + 2 * last):
        if tick < micro + last:
            made, *stores, w_in_near, w_out_near = forward_step(
                tick, micro, ctl, came, inputs, w_in_near, w_out_near, gain, stores
            )
            came = lax.ppermute(made, "section", onward)
        if tick >= last:
            made, *both, w_in_near, w_out_near = backward_step(
                tick, micro, last, ctl, arriving, cotangent, w_in_near, w_out_near, gain, stores, kept
            )
            stores, kept = both[:2], both[2:]
            arriving = lax.ppermute(made, "section", back)
    rows_wide = spread(stores[0][:micro].reshape(tokens, width))
    up_wide = spread(kept[0][:micro].reshape(tokens, width)).reshape(chips * tokens, -1)
    pair = kept[1][:micro].reshape(1, tokens, 2 * hidden)
    pair_wide = lax.all_to_all(
        jnp.broadcast_to(pair, (chips, tokens, 2 * hidden)), CHIPS, split_axis=0, concat_axis=0, tiled=True
    ).reshape(chips * tokens, -1)
    rows_wide = rows_wide.reshape(chips * tokens, -1)

    def column_product(left, right):
        return lax.dot_general(
            left, right, (((0,), (0,)), ((), ())), preferred_element_type=jnp.float32
        )

    half = rows_wide.shape[1] // 2
    core = lax.axis_index(CORE)
    partial = jnp.concatenate(
        [column_product(rows_wide, pair_wide[:, :hidden]), column_product(up_wide, pair_wide[:, hidden:])],
        axis=1,
    )
    mine = lax.dynamic_slice_in_dim(partial, core * half, half, 0)
    theirs = lax.dynamic_slice_in_dim(partial, (1 - core) * half, half, 0).astype(jnp.bfloat16)
    total = mine + lax.ppermute(theirs, CORE, [(0, 1), (1, 0)]).astype(jnp.float32)
    plain = total[:, :hidden]
    low = lax.axis_index(DP) * half
    gain_cut = lax.dynamic_slice_in_dim(gain[0], low, half, 0)
    w_cut = lax.dynamic_slice_in_dim(w_in, low, half, 0).astype(jnp.float32)
    in_grad = plain * gain_cut[:, None]
    gain_grad = jnp.sum(plain * w_cut, axis=1)
    return (in_grad[None], total[None, :, hidden:], gain_grad[None])


def solution(mesh):
    finer = Mesh(
        mesh.devices.reshape(2, 4, 2, mesh.shape["section"]), ("dp_0", "dp_1", "dp_2", "section")
    )
    in_specs = (
        P(DP, None),
        P(DP, None),
        P("section", None, None),
        P("section", None, None),
        P("section", None),
    )
    out_specs = (P("section", DP, None), P("section", DP, None), P("section", DP))
    return jax.shard_map(local, mesh=finer, in_specs=in_specs, out_specs=out_specs, check_vma=False)
```

```python
import functools

import jax
import jax.numpy as jnp
from jax import lax
from jax.experimental import pallas as pl
from jax.experimental.pallas import tpu as pltpu
from jax.sharding import Mesh
from jax.sharding import PartitionSpec as P

ROWS = 16
EARLY = 7
WAIT = 4
UNROLL = 8
SCOPED = 6 << 20
DP = ("dp_0", "dp_1", "dp_2")
CHIPS = ("dp_0", "dp_1")
CORE = "dp_2"
EPSILON = 1e-05

VMEM = pl.BlockSpec(memory_space=pltpu.VMEM)
SMEM = pl.BlockSpec(memory_space=pltpu.SMEM)
HBM = pl.BlockSpec(memory_space=pltpu.HBM)


def bring_in(low, micro, mine, came_ref, source_ref, rows_ref, sem):
    def fetch():
        copy = pltpu.make_async_copy(source_ref.at[pl.ds(low * ROWS, ROWS), :], rows_ref, sem)
        copy.start()
        copy.wait()

    if came_ref is None:
        fetch()
    elif not 0 <= low < micro:
        rows_ref[...] = came_ref[...]
    else:
        pl.when(mine)(fetch)

        @pl.when(jnp.logical_not(mine))
        def _():
            rows_ref[...] = came_ref[...]


def turned(k, ctl_ref, pieces):
    away = k - ctl_ref[ctl_ref.shape[0] - 3]
    return jnp.where(away < 0, away + pieces, away)


def column_cut(k, size):
    return pl.ds(pl.multiple_of(k * size, size), size)


def forward_body(tick, micro, *refs):
    starting = tick == 0
    ctl_ref, source_ref, w_in_far, w_out_far, gain_ref, *refs = refs
    came_ref = None if starting else refs[0]
    (out_ref, rows_all, pre_all, w_in_ref, w_out_ref, rows_ref, source_sem, load_sem) = refs[-8:]
    width, hidden = w_in_ref.shape
    pieces, _, _, size = rows_all.shape
    slot = ctl_ref[tick]

    def load(which, k):
        far, near = ((w_in_far, w_in_ref), (w_out_far, w_out_ref))[which]
        cut = column_cut(k, size)
        return pltpu.make_async_copy(far.at[cut, :], near.at[cut, :], load_sem.at[which, k])

    if starting:
        for which in range(2):
            for k in range(pieces):
                load(which, k).start()
    mine = ctl_ref[ctl_ref.shape[0] - 2] == 1
    bring_in(tick, micro, mine, came_ref, source_ref, rows_ref, source_sem)

    def project(k, carry):
        pre, total = carry
        if starting:
            load(0, k).wait()
        cut = column_cut(k, size)
        rows = rows_ref[:, cut]
        rows_all[turned(k, ctl_ref, pieces), slot] = rows
        rows = rows.astype(jnp.float32)
        pre = pre + jnp.dot(
            (rows * gain_ref[:, cut]).astype(jnp.bfloat16), w_in_ref[cut, :], preferred_element_type=jnp.float32
        )
        return pre, total + jnp.sum(rows * rows, axis=1, keepdims=True)

    zeros = jnp.zeros((ROWS, hidden), jnp.float32), jnp.zeros((ROWS, 1), jnp.float32)
    pre, total = lax.fori_loop(0, pieces, project, zeros, unroll=UNROLL)
    row_scale = lax.rsqrt(total / width + EPSILON)
    pre = pre * row_scale
    pre_all[slot, :, :hidden] = pre
    pre_all[slot, :, hidden:] = jnp.broadcast_to(row_scale, (ROWS, 128))
    act = (pre * jax.nn.sigmoid(pre)).astype(jnp.bfloat16)

    def expand(k, carry):
        if starting:
            load(1, k).wait()
        cut = column_cut(k, size)
        branch = lax.dot_general(
            act, w_out_ref[cut, :], (((1,), (1,)), ((), ())), preferred_element_type=jnp.float32
        )
        out_ref[:, cut] = (rows_ref[:, cut].astype(jnp.float32) + branch).astype(jnp.bfloat16)
        return carry

    lax.fori_loop(0, pieces, expand, 0, unroll=UNROLL)


def forward_step(tick, micro, pieces, ctl, source, w_in, w_out, gain, came, stores):
    width, hidden = w_in.shape
    starting = tick == 0
    weight = HBM if starting else VMEM
    return pl.pallas_call(
        functools.partial(forward_body, tick, micro),
        out_shape=(
            jax.ShapeDtypeStruct((ROWS, width), jnp.bfloat16),
            pltpu.VMEM((pieces, micro + 1, ROWS, width // pieces), jnp.bfloat16),
            pltpu.VMEM((micro + 1, ROWS, hidden + 128), jnp.float32),
            pltpu.VMEM(w_in.shape, jnp.bfloat16),
            pltpu.VMEM(w_out.shape, jnp.bfloat16),
        ),
        in_specs=[SMEM, HBM, weight, weight, VMEM] + [VMEM] * (0 if starting else 3),
        out_specs=(VMEM,) * 5,
        scratch_shapes=[
            pltpu.VMEM((ROWS, width), jnp.bfloat16),
            pltpu.SemaphoreType.DMA,
            pltpu.SemaphoreType.DMA((2, pieces)),
        ],
        input_output_aliases={} if starting else {2: 3, 3: 4, 6: 1, 7: 2},
        compiler_params=pltpu.CompilerParams(vmem_limit_bytes=SCOPED),
        name="forward_step",
    )(ctl, source, w_in, w_out, gain, *(() if starting else (came, *stores)))


def backward_body(tick, micro, last, *refs):
    starting = tick == last
    ctl_ref, source_ref, w_in_in, w_out_in, gain_ref, rows_in, pre_in, *refs = refs
    came_ref = None if starting else refs[0]
    (out_ref, rows_all, pre_all, both_all, w_in_ref, w_out_ref, up_ref, sem) = refs[-8:]
    width, hidden = w_in_ref.shape
    pieces, _, _, size = rows_all.shape
    slot = ctl_ref[micro + tick]
    mine = ctl_ref[ctl_ref.shape[0] - 1] == 1
    bring_in(tick - last, micro, mine, came_ref, source_ref, up_ref, sem)

    def project(k, total):
        cut = column_cut(k, size)
        up = up_ref[:, cut]
        both_all[turned(k, ctl_ref, pieces), slot, :, :size] = up
        return total + jnp.dot(up, w_out_ref[cut, :], preferred_element_type=jnp.float32)

    grad_act = lax.fori_loop(0, pieces, project, jnp.zeros((ROWS, hidden), jnp.float32), unroll=UNROLL)
    pre = pre_all[slot, :, :hidden]
    row_scale = pre_all[slot, :, hidden : hidden + 1]
    sig = jax.nn.sigmoid(pre)
    grad_pre = grad_act * sig * (1.0 + pre * (1.0 - sig))
    scaled = (grad_pre * row_scale).astype(jnp.bfloat16)
    act = (pre * sig).astype(jnp.bfloat16)
    for k in range(pieces):
        both_all[k, slot, :, size : size + hidden] = scaled
        both_all[k, slot, :, size + hidden :] = act
    pull = jnp.sum(scaled.astype(jnp.float32) * pre, axis=1, keepdims=True) * row_scale / width

    def expand(k, carry):
        cut = column_cut(k, size)
        grad_norm = lax.dot_general(
            scaled, w_in_ref[cut, :], (((1,), (1,)), ((), ())), preferred_element_type=jnp.float32
        )
        out_ref[:, cut] = (
            up_ref[:, cut].astype(jnp.float32)
            + grad_norm * gain_ref[:, cut]
            - rows_all[turned(k, ctl_ref, pieces), slot].astype(jnp.float32) * pull
        ).astype(jnp.bfloat16)
        return carry

    lax.fori_loop(0, pieces, expand, 0, unroll=UNROLL)


def backward_step(tick, micro, last, pieces, ctl, source, w_in, w_out, gain, stores, came, kept):
    width, hidden = w_in.shape
    starting = tick == last
    size = width // pieces
    return pl.pallas_call(
        functools.partial(backward_body, tick, micro, last),
        out_shape=(
            jax.ShapeDtypeStruct((ROWS, width), jnp.bfloat16),
            pltpu.VMEM((pieces, micro + 1, ROWS, size), jnp.bfloat16),
            pltpu.VMEM((micro + 1, ROWS, hidden + 128), jnp.float32),
            pltpu.VMEM((pieces, micro + 1, ROWS, size + 2 * hidden), jnp.bfloat16),
            pltpu.VMEM(w_in.shape, jnp.bfloat16),
            pltpu.VMEM(w_out.shape, jnp.bfloat16),
        ),
        in_specs=[SMEM, HBM] + [VMEM] * (5 if starting else 7),
        out_specs=(VMEM,) * 6,
        scratch_shapes=[pltpu.VMEM((ROWS, width), jnp.bfloat16), pltpu.SemaphoreType.DMA],
        input_output_aliases={2: 4, 3: 5, 5: 1, 6: 2, **({} if starting else {8: 3})},
        compiler_params=pltpu.CompilerParams(vmem_limit_bytes=SCOPED),
        name="backward_step",
    )(ctl, source, w_in, w_out, gain, *stores, *(() if starting else (came, kept)))


def gradient_body(counts, span, ctl_ref, *refs):
    parts, adding, splitting = counts
    sources, refs = refs[: 2 * parts], refs[2 * parts :]
    rows_buf, both_buf, sems = refs[-3:]
    copies = []
    each = span[1] - span[0]
    for k, source in enumerate(sources):
        buf = rows_buf if k < parts else both_buf
        source = source.at[pl.ds(span[0], each), :] if k < parts else source
        at = pl.ds(k % parts * each, each)
        copies.append(pltpu.make_async_copy(source, buf.at[at, :], sems.at[k]))
    for copy in copies:
        copy.start()
    for copy in copies:
        copy.wait()
    size = rows_buf.shape[1]
    hidden = (both_buf.shape[1] - size) // 2
    core = ctl_ref[ctl_ref.shape[0] - 4]

    def product(left, right):
        return lax.dot_general(left, right, (((0,), (0,)), ((), ())), preferred_element_type=jnp.float32)

    half = size // 2
    for which in range(2):
        low = pl.multiple_of((core if which == 0 else 1 - core) * half, half) if splitting else which * half
        rows = rows_buf[:, pl.ds(low, half)]
        ups = both_buf[:, pl.ds(low, half)]
        for side, value in enumerate(
            (product(rows, both_buf[:, size : size + hidden]), product(ups, both_buf[:, size + hidden :]))
        ):
            at = slice(side * hidden, (side + 1) * hidden)
            if adding:
                value = value + refs[0][pl.ds(low, half), at]
            if splitting:
                out_ref = refs[adding + which]
                out_ref[:, at] = value.astype(out_ref.dtype)
            else:
                refs[adding][pl.ds(low, half), at] = value


def gradient_step(ctl, rows, both, span, before, splitting):
    size = rows[0].shape[1]
    each = span[1] - span[0]
    pair = both[0].shape[1] - size
    tokens = each * len(rows)
    if splitting:
        out_shape = (
            jax.ShapeDtypeStruct((size // 2, pair), jnp.float32),
            jax.ShapeDtypeStruct((size // 2, pair), jnp.bfloat16),
        )
    else:
        out_shape = (jax.ShapeDtypeStruct((size, pair), jnp.float32),)
    adding = 0 if before is None else 1
    return pl.pallas_call(
        functools.partial(gradient_body, (len(rows), adding, splitting), span),
        out_shape=out_shape,
        in_specs=[SMEM] + [pl.BlockSpec(memory_space=pl.ANY)] * (2 * len(rows)) + [VMEM] * adding,
        out_specs=(VMEM,) * len(out_shape),
        scratch_shapes=[
            pltpu.VMEM((tokens, size), jnp.bfloat16),
            pltpu.VMEM((tokens, size + pair), jnp.bfloat16),
            pltpu.SemaphoreType.DMA((2 * len(rows),)),
        ],
        compiler_params=pltpu.CompilerParams(vmem_limit_bytes=26 << 20),
        name="gradient_step",
    )(ctl, *rows, *both, *(() if before is None else (before,)))


def finish_body(mine_ref, came_ref, w_ref, gain_ref, in_ref, out_ref, sum_ref):
    hidden = in_ref.shape[1]
    total = mine_ref[...] + came_ref[...].astype(jnp.float32)
    plain = total[:, :hidden]
    in_ref[...] = plain * gain_ref[:, :1]
    out_ref[...] = total[:, hidden:]
    sum_ref[...] = jnp.sum(plain * w_ref[...].astype(jnp.float32), axis=1, keepdims=True)


def local(inputs, cotangent, weight_in, weight_out, norm_gains):
    gain = norm_gains
    tokens, width = inputs.shape
    hidden = weight_in.shape[2]
    micro = tokens // ROWS
    sections = lax.axis_size("section")
    last = sections - 1
    pos = lax.axis_index("section")
    chips = lax.axis_size(CHIPS)
    half = width // (chips * lax.axis_size(CORE))
    onward = [(i, (i + 1) % sections) for i in range(sections)]
    back = [((i + 1) % sections, i) for i in range(sections)]
    ticks = jnp.arange(micro + last)
    which = jnp.concatenate([ticks - pos, ticks - last + pos])
    slots = jnp.where((which >= 0) & (which < micro), which, micro)
    own = jnp.stack([lax.axis_index(CORE), lax.axis_index(CHIPS), pos == 0, pos == last])
    ctl = jnp.concatenate([slots, own]).astype(jnp.int32)
    low = lax.axis_index(DP) * half
    gain_cut = jnp.broadcast_to(lax.dynamic_slice_in_dim(gain[0], low, half, 0)[:, None], (half, 128))
    w_cut = lax.dynamic_slice_in_dim(weight_in[0], low, half, 0)
    ctl, gain_cut, w_cut, inputs, cotangent, w_in_near, w_out_near = lax.optimization_barrier(
        (ctl, gain_cut, w_cut, inputs, cotangent, weight_in[0], weight_out[0])
    )
    inputs, cotangent, w_in_near, w_out_near = (
        pltpu.with_memory_space_constraint(array, pltpu.HBM)
        for array in (inputs, cotangent, w_in_near, w_out_near)
    )

    def hand_round(tiles):
        tiles = tiles.reshape(chips, -1, tiles.shape[-1])
        return [tiles[0]] + [
            lax.ppermute(tiles[d], CHIPS, [(i, (i + d) % chips) for i in range(chips)]) for d in range(1, chips)
        ]

    def by_now(array, others):
        array, *others = lax.optimization_barrier((array, *others))
        return array, others

    stores = kept = came = arriving = None
    rows_all = both_early = None
    for tick in range(micro + 2 * last):
        if tick < micro + last:
            made, *stores, w_in_near, w_out_near = forward_step(
                tick, micro, chips, ctl, inputs, w_in_near, w_out_near, gain, came, stores
            )
            came = lax.ppermute(made, "section", onward)
        if tick == micro - 1 + last:
            rows_all = hand_round(stores[0][:, :micro])
        if tick == micro - 1 + last + WAIT:
            arriving, rows_all = by_now(arriving, rows_all)
        if tick >= last:
            made, *stores, kept, w_in_near, w_out_near = backward_step(
                tick, micro, last, chips, ctl, cotangent, w_in_near, w_out_near, gain, stores, arriving, kept
            )
            if tick < micro + 2 * last - 1:
                arriving = lax.ppermute(made, "section", back)
        if tick == EARLY - 1 + 2 * last:
            both_early = hand_round(kept[:, :EARLY])
    cut = EARLY * ROWS
    (before,) = gradient_step(ctl, rows_all, both_early, (0, cut), None, False)
    both_late = hand_round(kept[:, EARLY:micro])
    mine, theirs = gradient_step(ctl, rows_all, both_late, (cut, tokens), before, True)
    theirs = lax.ppermute(theirs, CORE, [(0, 1), (1, 0)])
    in_grad, out_grad, gain_grad = pl.pallas_call(
        finish_body,
        out_shape=(
            jax.ShapeDtypeStruct((half, hidden), jnp.float32),
            jax.ShapeDtypeStruct((half, hidden), jnp.float32),
            jax.ShapeDtypeStruct((half, 1), jnp.float32),
        ),
        in_specs=[VMEM] * 4,
        out_specs=(VMEM,) * 3,
        name="finish",
    )(mine, theirs, w_cut, gain_cut)
    return (in_grad[None], out_grad[None], gain_grad.reshape(1, half))


def solution(mesh):
    finer = Mesh(
        mesh.devices.reshape(2, 4, 2, mesh.shape["section"]), ("dp_0", "dp_1", "dp_2", "section")
    )
    in_specs = (
        P(DP, None),
        P(DP, None),
        P("section", None, None),
        P("section", None, None),
        P("section", None),
    )
    out_specs = (P("section", DP, None), P("section", DP, None), P("section", DP))
    return jax.shard_map(local, mesh=finer, in_specs=in_specs, out_specs=out_specs, check_vma=False)
```

```python
import functools

import jax
import jax.numpy as jnp
from jax import lax
from jax.experimental import pallas as pl
from jax.experimental.pallas import tpu as pltpu
from jax.sharding import Mesh
from jax.sharding import PartitionSpec as P

ROWS = 16
WAIT = 2
FIRST, SECOND = 4, 8
ROWS_AT = (7, 7, 7, 6, 6, 6, 5, 5)
FIRST_AT = (5, 5, 4, 4, 4, 3, 3, 3)
SECOND_AT = (2, 2, 2, 2, 1, 1, 1, 1)
UNROLL = 8
SCOPED = 6 << 20
DP = ("dp_0", "dp_1", "dp_2")
CHIPS = ("dp_0", "dp_1")
CORE = "dp_2"
EPSILON = 1e-05

VMEM = pl.BlockSpec(memory_space=pltpu.VMEM)
SMEM = pl.BlockSpec(memory_space=pltpu.SMEM)
HBM = pl.BlockSpec(memory_space=pltpu.HBM)


def bring_in(low, micro, mine, came_ref, source_ref, rows_ref, sem):
    def fetch():
        copy = pltpu.make_async_copy(source_ref.at[pl.ds(low * ROWS, ROWS), :], rows_ref, sem)
        copy.start()
        copy.wait()

    if came_ref is None:
        fetch()
    elif not 0 <= low < micro:
        rows_ref[...] = came_ref[...]
    else:
        pl.when(mine)(fetch)

        @pl.when(jnp.logical_not(mine))
        def _():
            rows_ref[...] = came_ref[...]


def turned(k, ctl_ref, pieces):
    away = k - ctl_ref[ctl_ref.shape[0] - 3]
    return jnp.where(away < 0, away + pieces, away)


def column_cut(k, size):
    return pl.ds(pl.multiple_of(k * size, size), size)


def forward_body(tick, micro, *refs):
    starting = tick == 0
    ctl_ref, source_ref, w_in_far, w_out_far, gain_ref, *refs = refs
    came_ref = None if starting else refs[0]
    (out_ref, rows_all, pre_all, w_in_ref, w_out_ref, rows_ref, source_sem, load_sem) = refs[-8:]
    width, hidden = w_in_ref.shape
    pieces, _, _, size = rows_all.shape
    slot = ctl_ref[tick]

    def load(which, k):
        far, near = ((w_in_far, w_in_ref), (w_out_far, w_out_ref))[which]
        cut = column_cut(k, size)
        return pltpu.make_async_copy(far.at[cut, :], near.at[cut, :], load_sem.at[which, k])

    if starting:
        for which in range(2):
            for k in range(pieces):
                load(which, k).start()
    mine = ctl_ref[ctl_ref.shape[0] - 2] == 1
    bring_in(tick, micro, mine, came_ref, source_ref, rows_ref, source_sem)

    def project(k, carry):
        pre, total = carry
        if starting:
            load(0, k).wait()
        cut = column_cut(k, size)
        rows = rows_ref[:, cut]
        rows_all[turned(k, ctl_ref, pieces), slot] = rows
        rows = rows.astype(jnp.float32)
        pre = pre + jnp.dot(
            (rows * gain_ref[:, cut]).astype(jnp.bfloat16), w_in_ref[cut, :], preferred_element_type=jnp.float32
        )
        return pre, total + jnp.sum(rows * rows, axis=1, keepdims=True)

    zeros = jnp.zeros((ROWS, hidden), jnp.float32), jnp.zeros((ROWS, 1), jnp.float32)
    pre, total = lax.fori_loop(0, pieces, project, zeros, unroll=UNROLL)
    row_scale = lax.rsqrt(total / width + EPSILON)
    pre = pre * row_scale
    pre_all[slot, :, :hidden] = pre
    pre_all[slot, :, hidden:] = jnp.broadcast_to(row_scale, (ROWS, 128))
    act = (pre * jax.nn.sigmoid(pre)).astype(jnp.bfloat16)

    def expand(k, carry):
        if starting:
            load(1, k).wait()
        cut = column_cut(k, size)
        branch = lax.dot_general(
            act, w_out_ref[cut, :], (((1,), (1,)), ((), ())), preferred_element_type=jnp.float32
        )
        out_ref[:, cut] = (rows_ref[:, cut].astype(jnp.float32) + branch).astype(jnp.bfloat16)
        return carry

    lax.fori_loop(0, pieces, expand, 0, unroll=UNROLL)


def forward_step(tick, micro, pieces, ctl, source, w_in, w_out, gain, came, stores):
    width, hidden = w_in.shape
    starting = tick == 0
    weight = HBM if starting else VMEM
    return pl.pallas_call(
        functools.partial(forward_body, tick, micro),
        out_shape=(
            jax.ShapeDtypeStruct((ROWS, width), jnp.bfloat16),
            pltpu.VMEM((pieces, micro + 1, ROWS, width // pieces), jnp.bfloat16),
            pltpu.VMEM((micro + 1, ROWS, hidden + 128), jnp.float32),
            pltpu.VMEM(w_in.shape, jnp.bfloat16),
            pltpu.VMEM(w_out.shape, jnp.bfloat16),
        ),
        in_specs=[SMEM, HBM, weight, weight, VMEM] + [VMEM] * (0 if starting else 3),
        out_specs=(VMEM,) * 5,
        scratch_shapes=[
            pltpu.VMEM((ROWS, width), jnp.bfloat16),
            pltpu.SemaphoreType.DMA,
            pltpu.SemaphoreType.DMA((2, pieces)),
        ],
        input_output_aliases={} if starting else {2: 3, 3: 4, 6: 1, 7: 2},
        compiler_params=pltpu.CompilerParams(vmem_limit_bytes=SCOPED),
        name="forward_step",
    )(ctl, source, w_in, w_out, gain, *(() if starting else (came, *stores)))


def backward_body(tick, micro, last, *refs):
    starting = tick == last
    ctl_ref, source_ref, w_in_in, w_out_in, gain_ref, rows_in, pre_in, *refs = refs
    came_ref = None if starting else refs[0]
    (out_ref, rows_all, pre_all, both_all, w_in_ref, w_out_ref, up_ref, sem) = refs[-8:]
    width, hidden = w_in_ref.shape
    pieces, _, _, size = rows_all.shape
    slot = ctl_ref[micro + tick]
    mine = ctl_ref[ctl_ref.shape[0] - 1] == 1
    bring_in(tick - last, micro, mine, came_ref, source_ref, up_ref, sem)

    def project(k, total):
        cut = column_cut(k, size)
        up = up_ref[:, cut]
        both_all[turned(k, ctl_ref, pieces), slot, :, :size] = up
        return total + jnp.dot(up, w_out_ref[cut, :], preferred_element_type=jnp.float32)

    grad_act = lax.fori_loop(0, pieces, project, jnp.zeros((ROWS, hidden), jnp.float32), unroll=UNROLL)
    pre = pre_all[slot, :, :hidden]
    row_scale = pre_all[slot, :, hidden : hidden + 1]
    sig = jax.nn.sigmoid(pre)
    grad_pre = grad_act * sig * (1.0 + pre * (1.0 - sig))
    scaled = (grad_pre * row_scale).astype(jnp.bfloat16)
    act = (pre * sig).astype(jnp.bfloat16)
    for k in range(pieces):
        both_all[k, slot, :, size : size + hidden] = scaled
        both_all[k, slot, :, size + hidden :] = act
    pull = jnp.sum(scaled.astype(jnp.float32) * pre, axis=1, keepdims=True) * row_scale / width

    def expand(k, carry):
        cut = column_cut(k, size)
        grad_norm = lax.dot_general(
            scaled, w_in_ref[cut, :], (((1,), (1,)), ((), ())), preferred_element_type=jnp.float32
        )
        out_ref[:, cut] = (
            up_ref[:, cut].astype(jnp.float32)
            + grad_norm * gain_ref[:, cut]
            - rows_all[turned(k, ctl_ref, pieces), slot].astype(jnp.float32) * pull
        ).astype(jnp.bfloat16)
        return carry

    lax.fori_loop(0, pieces, expand, 0, unroll=UNROLL)


def backward_step(tick, micro, last, pieces, ctl, source, w_in, w_out, gain, stores, came, kept):
    width, hidden = w_in.shape
    starting = tick == last
    size = width // pieces
    return pl.pallas_call(
        functools.partial(backward_body, tick, micro, last),
        out_shape=(
            jax.ShapeDtypeStruct((ROWS, width), jnp.bfloat16),
            pltpu.VMEM((pieces, micro + 1, ROWS, size), jnp.bfloat16),
            pltpu.VMEM((micro + 1, ROWS, hidden + 128), jnp.float32),
            pltpu.VMEM((pieces, micro + 1, ROWS, size + 2 * hidden), jnp.bfloat16),
            pltpu.VMEM(w_in.shape, jnp.bfloat16),
            pltpu.VMEM(w_out.shape, jnp.bfloat16),
        ),
        in_specs=[SMEM, HBM] + [VMEM] * (5 if starting else 7),
        out_specs=(VMEM,) * 6,
        scratch_shapes=[pltpu.VMEM((ROWS, width), jnp.bfloat16), pltpu.SemaphoreType.DMA],
        input_output_aliases={2: 4, 3: 5, 5: 1, 6: 2, **({} if starting else {8: 3})},
        compiler_params=pltpu.CompilerParams(vmem_limit_bytes=SCOPED),
        name="backward_step",
    )(ctl, source, w_in, w_out, gain, *stores, *(() if starting else (came, kept)))


def gradient_body(plan, ctl_ref, *refs):
    parts, span, groups, adding, splitting = plan
    sources, refs = refs[: parts * (1 + groups)], refs[parts * (1 + groups) :]
    rows_buf, both_buf, sems = refs[-3:]
    each = span[1] - span[0]
    copies = []
    for k in range(parts):
        source = sources[k].at[pl.ds(span[0], each), :]
        copies.append(pltpu.make_async_copy(source, rows_buf.at[pl.ds(k * each, each), :], sems.at[k]))
        high = k * each
        for g in range(groups):
            source = sources[parts * (1 + g) + k]
            at = pl.ds(high, source.shape[0])
            copies.append(pltpu.make_async_copy(source, both_buf.at[at, :], sems.at[parts * (1 + g) + k]))
            high += source.shape[0]
    for copy in copies:
        copy.start()
    for copy in copies:
        copy.wait()
    size = rows_buf.shape[1]
    hidden = (both_buf.shape[1] - size) // 2
    core = ctl_ref[ctl_ref.shape[0] - 4]

    def product(left, right):
        return lax.dot_general(left, right, (((0,), (0,)), ((), ())), preferred_element_type=jnp.float32)

    half = size // 2
    for which in range(2):
        low = pl.multiple_of((core if which == 0 else 1 - core) * half, half) if splitting else which * half
        rows = rows_buf[:, pl.ds(low, half)]
        ups = both_buf[:, pl.ds(low, half)]
        for side, value in enumerate(
            (product(rows, both_buf[:, size : size + hidden]), product(ups, both_buf[:, size + hidden :]))
        ):
            at = slice(side * hidden, (side + 1) * hidden)
            if adding:
                value = value + refs[0][pl.ds(low, half), at]
            if splitting:
                out_ref = refs[adding + which]
                out_ref[:, at] = value.astype(out_ref.dtype)
            else:
                refs[adding][pl.ds(low, half), at] = value


def gradient_step(ctl, rows, span, groups, before, splitting):
    size = rows[0].shape[1]
    pair = groups[0][0].shape[1] - size
    tokens = (span[1] - span[0]) * len(rows)
    if splitting:
        out_shape = (
            jax.ShapeDtypeStruct((size // 2, pair), jnp.float32),
            jax.ShapeDtypeStruct((size // 2, pair), jnp.bfloat16),
        )
    else:
        out_shape = (jax.ShapeDtypeStruct((size, pair), jnp.float32),)
    adding = 0 if before is None else 1
    count = len(rows) * (1 + len(groups))
    return pl.pallas_call(
        functools.partial(gradient_body, (len(rows), span, len(groups), adding, splitting)),
        out_shape=out_shape,
        in_specs=[SMEM] + [pl.BlockSpec(memory_space=pl.ANY)] * count + [VMEM] * adding,
        out_specs=(VMEM,) * len(out_shape),
        scratch_shapes=[
            pltpu.VMEM((tokens, size), jnp.bfloat16),
            pltpu.VMEM((tokens, size + pair), jnp.bfloat16),
            pltpu.SemaphoreType.DMA((count,)),
        ],
        compiler_params=pltpu.CompilerParams(vmem_limit_bytes=20 << 20),
        name="gradient_step",
    )(ctl, *rows, *(piece for group in groups for piece in group), *(() if before is None else (before,)))


def finish_body(mine_ref, came_ref, w_ref, gain_ref, in_ref, out_ref, sum_ref):
    hidden = in_ref.shape[1]
    total = mine_ref[...] + came_ref[...].astype(jnp.float32)
    plain = total[:, :hidden]
    in_ref[...] = plain * gain_ref[:, :1]
    out_ref[...] = total[:, hidden:]
    ones = jnp.ones((8, hidden), jnp.float32)
    sum_ref[...] = lax.dot_general(
        ones,
        plain * w_ref[...].astype(jnp.float32),
        (((1,), (1,)), ((), ())),
        precision=lax.Precision.HIGHEST,
        preferred_element_type=jnp.float32,
    )[:1]


def local(inputs, cotangent, weight_in, weight_out, norm_gains):
    gain = norm_gains
    tokens, width = inputs.shape
    hidden = weight_in.shape[2]
    micro = tokens // ROWS
    sections = lax.axis_size("section")
    last = sections - 1
    pos = lax.axis_index("section")
    chips = lax.axis_size(CHIPS)
    half = width // (chips * lax.axis_size(CORE))
    onward = [(i, (i + 1) % sections) for i in range(sections)]
    back = [((i + 1) % sections, i) for i in range(sections)]
    ticks = jnp.arange(micro + last)
    which = jnp.concatenate([ticks - pos, ticks - last + pos])
    slots = jnp.where((which >= 0) & (which < micro), which, micro)
    own = jnp.stack([lax.axis_index(CORE), lax.axis_index(CHIPS), pos == 0, pos == last])
    ctl = jnp.concatenate([slots, own]).astype(jnp.int32)
    low = lax.axis_index(DP) * half
    gain_cut = jnp.broadcast_to(lax.dynamic_slice_in_dim(gain[0], low, half, 0)[:, None], (half, 128))
    w_cut = lax.dynamic_slice_in_dim(weight_in[0], low, half, 0)
    ctl, gain_cut, w_cut, inputs, cotangent, w_in_near, w_out_near = lax.optimization_barrier(
        (ctl, gain_cut, w_cut, inputs, cotangent, weight_in[0], weight_out[0])
    )
    inputs, cotangent, w_in_near, w_out_near = (
        pltpu.with_memory_space_constraint(array, pltpu.HBM)
        for array in (inputs, cotangent, w_in_near, w_out_near)
    )

    def shift(tile, d):
        tile = tile.reshape(-1, tile.shape[-1])
        return lax.ppermute(tile, CHIPS, [(i, (i + d) % chips) for i in range(chips)]) if d else tile

    groups = {"rows": (0, micro), "first": (0, FIRST), "second": (FIRST, SECOND), "third": (SECOND, micro)}
    sent = {name: [None] * chips for name in groups}
    leaving = {}
    end = micro + 2 * last - 1
    for name, when in (
        ("rows", ROWS_AT),
        ("first", FIRST_AT),
        ("second", SECOND_AT),
        ("third", (0,) * chips),
    ):
        for d, back_by in enumerate(when):
            leaving.setdefault(end - back_by, []).append((name, d))

    stores = kept = came = arriving = None
    for tick in range(micro + 2 * last):
        if tick < micro + last:
            made, *stores, w_in_near, w_out_near = forward_step(
                tick, micro, chips, ctl, inputs, w_in_near, w_out_near, gain, came, stores
            )
            came = lax.ppermute(made, "section", onward)
        due = leaving.get(tick - WAIT, ()) if tick >= last else ()
        if due:
            arriving, *pieces = lax.optimization_barrier((arriving, *(sent[name][d] for name, d in due)))
            for (name, d), piece in zip(due, pieces):
                sent[name][d] = piece
        if tick >= last:
            made, *stores, kept, w_in_near, w_out_near = backward_step(
                tick, micro, last, chips, ctl, cotangent, w_in_near, w_out_near, gain, stores, arriving, kept
            )
            if tick < end:
                arriving = lax.ppermute(made, "section", back)
            for name, d in leaving.get(tick, ()):
                low, high = groups[name]
                store = stores[0] if name == "rows" else kept
                sent[name][d] = shift(store[d, low:high], d)
    cut = SECOND * ROWS
    (before,) = gradient_step(ctl, sent["rows"], (0, cut), (sent["first"], sent["second"]), None, False)
    mine, theirs = gradient_step(ctl, sent["rows"], (cut, tokens), (sent["third"],), before, True)
    theirs = lax.ppermute(theirs, CORE, [(0, 1), (1, 0)])
    in_grad, out_grad, gain_grad = pl.pallas_call(
        finish_body,
        out_shape=(
            jax.ShapeDtypeStruct((half, hidden), jnp.float32),
            jax.ShapeDtypeStruct((half, hidden), jnp.float32),
            jax.ShapeDtypeStruct((1, half), jnp.float32),
        ),
        in_specs=[VMEM] * 4,
        out_specs=(VMEM,) * 3,
        compiler_params=pltpu.CompilerParams(vmem_limit_bytes=12 << 20),
        name="finish",
    )(mine, theirs, w_cut, gain_cut)
    return (in_grad[None], out_grad[None], gain_grad)


def solution(mesh):
    finer = Mesh(
        mesh.devices.reshape(2, 4, 2, mesh.shape["section"]), ("dp_0", "dp_1", "dp_2", "section")
    )
    in_specs = (
        P(DP, None),
        P(DP, None),
        P("section", None, None),
        P("section", None, None),
        P("section", None),
    )
    out_specs = (P("section", DP, None), P("section", DP, None), P("section", DP))
    return jax.shard_map(local, mesh=finer, in_specs=in_specs, out_specs=out_specs, check_vma=False)
```

```python
import functools

import jax
import jax.numpy as jnp
from jax import lax
from jax.experimental import pallas as pl
from jax.experimental.pallas import tpu as pltpu
from jax.sharding import Mesh
from jax.sharding import PartitionSpec as P

ROWS = 16
WAIT = 2
FIRST, SECOND = 4, 8
ROWS_AT = (7, 7, 7, 6, 6, 6, 5, 5)
FIRST_AT = (5, 5, 4, 4, 4, 3, 3, 3)
SECOND_AT = (2, 2, 2, 2, 1, 1, 1, 1)
UNROLL = 8
FLIP = 2
SCOPED = 6 << 20
DP = ("dp_0", "dp_1", "dp_2")
CHIPS = ("dp_0", "dp_1")
CORE = "dp_2"
EPSILON = 1e-05

VMEM = pl.BlockSpec(memory_space=pltpu.VMEM)
SMEM = pl.BlockSpec(memory_space=pltpu.SMEM)
HBM = pl.BlockSpec(memory_space=pltpu.HBM)


def bring_in(low, micro, mine, came_ref, source_ref, rows_ref, sem):
    def fetch():
        copy = pltpu.make_async_copy(source_ref.at[pl.ds(low * ROWS, ROWS), :], rows_ref, sem)
        copy.start()
        copy.wait()

    if came_ref is None:
        fetch()
    elif not 0 <= low < micro:
        rows_ref[...] = came_ref[...]
    else:
        pl.when(mine)(fetch)

        @pl.when(jnp.logical_not(mine))
        def _():
            rows_ref[...] = came_ref[...]


def turned(k, ctl_ref):
    return jnp.bitwise_xor(ctl_ref[ctl_ref.shape[0] - 3], k)


def column_cut(k, size):
    return pl.ds(pl.multiple_of(k * size, size), size)


def forward_body(tick, micro, skipped, flipped, *refs):
    starting = tick == 0
    ctl_ref, source_ref, w_in_far, w_out_far, gain_ref, *refs = refs
    came_ref = None if starting else refs[0]
    (out_ref, rows_all, pre_all, w_in_ref, w_out_ref, rows_ref, source_sem, load_sem) = refs[-8:]
    width, hidden = w_in_ref.shape
    pieces, _, _, size = rows_all.shape
    slot = ctl_ref[tick]

    def load(which, k):
        far, near = ((w_in_far, w_in_ref), (w_out_far, w_out_ref))[which]
        cut = column_cut(k, size)
        return pltpu.make_async_copy(far.at[cut, :], near.at[cut, :], load_sem.at[which, k])

    if starting:
        for which in range(2):
            for k in range(pieces):
                load(which, k).start()
    mine = ctl_ref[ctl_ref.shape[0] - 2] == 1
    bring_in(tick, micro, mine, came_ref, source_ref, rows_ref, source_sem)

    def project(k, carry):
        pre, total = carry
        if starting:
            load(0, k).wait()
        cut = column_cut(k, size)
        rows = rows_ref[:, cut]
        rows_all[turned(k, ctl_ref), slot] = rows
        rows = rows.astype(jnp.float32)
        pre = pre + jnp.dot(
            (rows * gain_ref[:, cut]).astype(jnp.bfloat16), w_in_ref[cut, :], preferred_element_type=jnp.float32
        )
        return pre, total + jnp.sum(rows * rows, axis=1, keepdims=True)

    zeros = jnp.zeros((ROWS, hidden), jnp.float32), jnp.zeros((ROWS, 1), jnp.float32)
    pre, total = lax.fori_loop(0, pieces, project, zeros, unroll=UNROLL)
    row_scale = lax.rsqrt(total / width + EPSILON)
    pre = pre * row_scale
    pre_all[slot, :, :hidden] = pre
    pre_all[slot, :, hidden:] = jnp.broadcast_to(row_scale, (ROWS, 128))
    act = (pre * jax.nn.sigmoid(pre)).astype(jnp.bfloat16)
    if skipped:
        return

    def expand(k, carry):
        if starting:
            load(1, k).wait()
        cut = column_cut(k, size)
        if flipped:
            branch = jnp.dot(act, w_out_ref[:, cut], preferred_element_type=jnp.float32)
        else:
            branch = lax.dot_general(
                act, w_out_ref[cut, :], (((1,), (1,)), ((), ())), preferred_element_type=jnp.float32
            )
        out_ref[:, cut] = (rows_ref[:, cut].astype(jnp.float32) + branch).astype(jnp.bfloat16)
        return carry

    lax.fori_loop(0, pieces, expand, 0, unroll=UNROLL)


def forward_step(tick, micro, skipped, flipped, pieces, ctl, source, w_in, w_out, gain, came, stores):
    width, hidden = w_in.shape
    starting = tick == 0
    weight = HBM if starting else VMEM
    return pl.pallas_call(
        functools.partial(forward_body, tick, micro, skipped, flipped),
        out_shape=(
            jax.ShapeDtypeStruct((ROWS, width), jnp.bfloat16),
            pltpu.VMEM((pieces, micro + 1, ROWS, width // pieces), jnp.bfloat16),
            pltpu.VMEM((micro + 1, ROWS, hidden + 128), jnp.float32),
            pltpu.VMEM(w_in.shape, jnp.bfloat16),
            pltpu.VMEM(w_out.shape, jnp.bfloat16),
        ),
        in_specs=[SMEM, HBM, weight, weight, VMEM] + [VMEM] * (0 if starting else 3),
        out_specs=(VMEM,) * 5,
        scratch_shapes=[
            pltpu.VMEM((ROWS, width), jnp.bfloat16),
            pltpu.SemaphoreType.DMA,
            pltpu.SemaphoreType.DMA((2, pieces)),
        ],
        input_output_aliases={} if starting else {2: 3, 3: 4, 6: 1, 7: 2},
        compiler_params=pltpu.CompilerParams(vmem_limit_bytes=SCOPED),
        name="forward_step",
    )(ctl, source, w_in, w_out, gain, *(() if starting else (came, *stores)))


def flip_body(far_ref, near_ref, flat_ref):
    for low in range(0, far_ref.shape[0], 512):
        flat_ref[:, low : low + 512] = jnp.transpose(near_ref[low : low + 512, :])


def flip(weight):
    return pl.pallas_call(
        flip_body,
        out_shape=(pltpu.VMEM(weight.shape, weight.dtype), pltpu.VMEM(weight.shape[::-1], weight.dtype)),
        in_specs=[VMEM],
        out_specs=(VMEM, VMEM),
        input_output_aliases={0: 0},
        cost_estimate=pl.CostEstimate(flops=5_000_000_000, transcendentals=0, bytes_accessed=16_000_000),
        compiler_params=pltpu.CompilerParams(vmem_limit_bytes=SCOPED),
        name="flip",
    )(weight)


def backward_body(tick, micro, last, *refs):
    ends = micro + 2 * last - 1
    starting = tick == last
    ctl_ref, source_ref, w_in_in, w_out_in, gain_ref, rows_in, pre_in, *refs = refs
    came_ref = None if starting else refs[0]
    (out_ref, rows_all, pre_all, up_all, pair_all, w_in_ref, w_out_ref, up_ref, sem) = refs[-9:]
    width, hidden = w_out_ref.shape
    pieces, _, _, size = rows_all.shape
    slot = ctl_ref[micro + tick]
    mine = ctl_ref[ctl_ref.shape[0] - 1] == 1
    bring_in(tick - last, micro, mine, came_ref, source_ref, up_ref, sem)

    def project(k, total):
        cut = column_cut(k, size)
        up = up_ref[:, cut]
        up_all[turned(k, ctl_ref), slot] = up
        return total + jnp.dot(up, w_out_ref[cut, :], preferred_element_type=jnp.float32)

    grad_act = lax.fori_loop(0, pieces, project, jnp.zeros((ROWS, hidden), jnp.float32), unroll=UNROLL)
    pre = pre_all[slot, :, :hidden]
    row_scale = pre_all[slot, :, hidden : hidden + 1]
    sig = jax.nn.sigmoid(pre)
    grad_pre = grad_act * sig * (1.0 + pre * (1.0 - sig))
    scaled = (grad_pre * row_scale).astype(jnp.bfloat16)
    pair_all[slot, :, :hidden] = scaled
    pair_all[slot, :, hidden:] = (pre * sig).astype(jnp.bfloat16)
    if tick == ends:
        return
    pull = jnp.sum(scaled.astype(jnp.float32) * pre, axis=1, keepdims=True) * row_scale / width

    def expand(k, carry):
        cut = column_cut(k, size)
        grad_norm = jnp.dot(scaled, w_in_ref[:, cut], preferred_element_type=jnp.float32)
        out_ref[:, cut] = (
            up_ref[:, cut].astype(jnp.float32)
            + grad_norm * gain_ref[:, cut]
            - rows_all[turned(k, ctl_ref), slot].astype(jnp.float32) * pull
        ).astype(jnp.bfloat16)
        return carry

    lax.fori_loop(0, pieces, expand, 0, unroll=UNROLL)


def backward_step(tick, micro, last, pieces, ctl, source, w_in, w_out, gain, stores, came, kept):
    width, hidden = w_out.shape
    starting = tick == last
    size = width // pieces
    return pl.pallas_call(
        functools.partial(backward_body, tick, micro, last),
        out_shape=(
            jax.ShapeDtypeStruct((ROWS, width), jnp.bfloat16),
            pltpu.VMEM((pieces, micro + 1, ROWS, size), jnp.bfloat16),
            pltpu.VMEM((micro + 1, ROWS, hidden + 128), jnp.float32),
            pltpu.VMEM((pieces, micro + 1, ROWS, size), jnp.bfloat16),
            pltpu.VMEM((micro + 1, ROWS, 2 * hidden), jnp.bfloat16),
            pltpu.VMEM(w_in.shape, jnp.bfloat16),
            pltpu.VMEM(w_out.shape, jnp.bfloat16),
        ),
        in_specs=[SMEM, HBM] + [VMEM] * (5 if starting else 8),
        out_specs=(VMEM,) * 7,
        scratch_shapes=[pltpu.VMEM((ROWS, width), jnp.bfloat16), pltpu.SemaphoreType.DMA],
        input_output_aliases={2: 5, 3: 6, 5: 1, 6: 2, **({} if starting else {8: 3, 9: 4})},
        compiler_params=pltpu.CompilerParams(vmem_limit_bytes=SCOPED),
        name="backward_step",
    )(ctl, source, w_in, w_out, gain, *stores, *(() if starting else (came, *kept)))


def gradient_body(plan, counts, ctl_ref, *refs):
    adding, splitting = counts
    sources = 1 + max(entry[0] for entry in plan)
    sources, refs = refs[:sources], refs[sources:]
    *bufs, sems = refs[-4:]
    copies = [
        pltpu.make_async_copy(sources[k].at[pl.ds(low, size), :], bufs[which].at[pl.ds(at, size), :], sems.at[n])
        for n, (k, low, size, which, at) in enumerate(plan)
    ]
    for copy in copies:
        copy.start()
    for copy in copies:
        copy.wait()
    rows_buf, up_buf, pair_buf = bufs
    size = rows_buf.shape[1]
    hidden = pair_buf.shape[1] // 2
    core = ctl_ref[ctl_ref.shape[0] - 4]

    def product(left, right):
        return lax.dot_general(left, right, (((0,), (0,)), ((), ())), preferred_element_type=jnp.float32)

    half = size // 2
    for which in range(2):
        low = pl.multiple_of((core if which == 0 else 1 - core) * half, half) if splitting else which * half
        rows = rows_buf[:, pl.ds(low, half)]
        ups = up_buf[:, pl.ds(low, half)]
        for side, value in enumerate(
            (product(rows, pair_buf[:, :hidden]), product(ups, pair_buf[:, hidden:]))
        ):
            at = slice(side * hidden, (side + 1) * hidden)
            if adding:
                value = value + refs[0][pl.ds(low, half), at]
            if splitting:
                out_ref = refs[adding + which]
                out_ref[:, at] = value.astype(out_ref.dtype)
            else:
                refs[adding][pl.ds(low, half), at] = value


def gradient_step(ctl, groups, sent, span, before, splitting):
    low, high = span
    plan, sources = [], []
    for name, content in groups.items():
        used = False
        for d, piece in enumerate(sent[name]):
            base = 0
            for kind, first, stop in content:
                start, end = max(first, low), min(stop, high)
                if start < end:
                    at = (d * (high - low) + start - low) * ROWS
                    plan.append((len(sources) + d, base + (start - first) * ROWS, (end - start) * ROWS, kind, at))
                    used = True
                base += (stop - first) * ROWS
        if used:
            sources += sent[name]
    size = sources[0].shape[1]
    tokens = (high - low) * ROWS * len(sent[name])
    if splitting:
        out_shape = (
            jax.ShapeDtypeStruct((size // 2, size), jnp.float32),
            jax.ShapeDtypeStruct((size // 2, size), jnp.bfloat16),
        )
    else:
        out_shape = (jax.ShapeDtypeStruct((size, size), jnp.float32),)
    adding = 0 if before is None else 1
    return pl.pallas_call(
        functools.partial(gradient_body, tuple(plan), (adding, splitting)),
        out_shape=out_shape,
        in_specs=[SMEM] + [pl.BlockSpec(memory_space=pl.ANY)] * len(sources) + [VMEM] * adding,
        out_specs=(VMEM,) * len(out_shape),
        scratch_shapes=[pltpu.VMEM((tokens, size), jnp.bfloat16)] * 3 + [pltpu.SemaphoreType.DMA((len(plan),))],
        compiler_params=pltpu.CompilerParams(vmem_limit_bytes=20 << 20),
        name="gradient_step",
    )(ctl, *sources, *(() if before is None else (before,)))


def finish_body(mine_ref, came_ref, w_ref, gain_ref, in_ref, out_ref, sum_ref):
    hidden = in_ref.shape[1]
    total = mine_ref[...] + came_ref[...].astype(jnp.float32)
    plain = total[:, :hidden]
    in_ref[...] = plain * gain_ref[:, :1]
    out_ref[...] = total[:, hidden:]
    ones = jnp.ones((8, hidden), jnp.float32)
    sum_ref[...] = lax.dot_general(
        ones,
        plain * w_ref[...].astype(jnp.float32),
        (((1,), (1,)), ((), ())),
        precision=lax.Precision.HIGHEST,
        preferred_element_type=jnp.float32,
    )[:1]


def local(inputs, cotangent, weight_in, weight_out, norm_gains):
    gain = norm_gains
    tokens, width = inputs.shape
    hidden = weight_in.shape[2]
    micro = tokens // ROWS
    sections = lax.axis_size("section")
    last = sections - 1
    pos = lax.axis_index("section")
    chips = lax.axis_size(CHIPS)
    half = width // (chips * lax.axis_size(CORE))
    onward = [(i, (i + 1) % sections) for i in range(sections)]
    back = [((i + 1) % sections, i) for i in range(sections)]
    ticks = jnp.arange(micro + last)
    which = jnp.concatenate([ticks - pos, ticks - last + pos])
    slots = jnp.where((which >= 0) & (which < micro), which, micro)
    own = jnp.stack([lax.axis_index(CORE), lax.axis_index(CHIPS), pos == 0, pos == last])
    ctl = jnp.concatenate([slots, own]).astype(jnp.int32)
    low = lax.axis_index(DP) * half
    gain_cut = jnp.broadcast_to(lax.dynamic_slice_in_dim(gain[0], low, half, 0)[:, None], (half, 128))
    w_cut = lax.dynamic_slice_in_dim(weight_in[0], low, half, 0)
    ctl, gain_cut, w_cut, inputs, cotangent, w_in_near, w_out_near = lax.optimization_barrier(
        (ctl, gain_cut, w_cut, inputs, cotangent, weight_in[0], weight_out[0])
    )
    inputs, cotangent, w_in_near, w_out_near = (
        pltpu.with_memory_space_constraint(array, pltpu.HBM)
        for array in (inputs, cotangent, w_in_near, w_out_near)
    )

    def shift(tile, d):
        tile = tile.reshape(-1, tile.shape[-1])
        return lax.ppermute(tile, CHIPS, [(i, i ^ d) for i in range(chips)]) if d else tile

    groups = {
        "rows": ((0, 0, micro),),
        "first": ((1, 0, FIRST), (2, 0, FIRST)),
        "second": ((1, FIRST, SECOND), (2, FIRST, SECOND)),
        "third": ((1, SECOND, micro), (2, SECOND, micro)),
    }
    sent = {name: [None] * chips for name in groups}
    leaving = {}
    end = micro + 2 * last - 1
    for name, when in (
        ("rows", ROWS_AT),
        ("first", FIRST_AT),
        ("second", SECOND_AT),
        ("third", (0,) * chips),
    ):
        for d, back_by in enumerate(when):
            leaving.setdefault(end - back_by, []).append((name, d))

    stores = kept = came = arriving = None
    for tick in range(micro + 2 * last):
        if tick < micro + last:
            flipped = tick >= FLIP
            out = w_out_flat if flipped else w_out_near
            made, *stores, w_in_near, out = forward_step(
                tick, micro, tick == micro + last - 1, flipped, chips, ctl, inputs, w_in_near, out, gain, came, stores
            )
            if flipped:
                w_out_flat = out
            else:
                w_out_near = out
            came = lax.ppermute(made, "section", onward)
            if tick == FLIP - 2:
                w_out_near, w_out_flat = flip(w_out_near)
            if tick == FLIP - 1:
                w_in_near, w_in_flat = flip(w_in_near)
        due = leaving.get(tick - WAIT, ()) if tick >= last else ()
        if due:
            arriving, *pieces = lax.optimization_barrier((arriving, *(sent[name][d] for name, d in due)))
            for (name, d), piece in zip(due, pieces):
                sent[name][d] = piece
        if tick >= last:
            made, *both, w_in_flat, w_out_near = backward_step(
                tick, micro, last, chips, ctl, cotangent, w_in_flat, w_out_near, gain, stores, arriving, kept
            )
            stores, kept = both[:2], both[2:]
            if tick < end:
                arriving = lax.ppermute(made, "section", back)
            for name, d in leaving.get(tick, ()):
                sources = (stores[0][d], kept[0][d], kept[1])
                tiles = [sources[kind][low:high] for kind, low, high in groups[name]]
                sent[name][d] = shift(jnp.concatenate(tiles) if len(tiles) > 1 else tiles[0], d)
    (before,) = gradient_step(ctl, groups, sent, (0, SECOND), None, False)
    mine, theirs = gradient_step(ctl, groups, sent, (SECOND, micro), before, True)
    theirs = lax.ppermute(theirs, CORE, [(0, 1), (1, 0)])
    in_grad, out_grad, gain_grad = pl.pallas_call(
        finish_body,
        out_shape=(
            jax.ShapeDtypeStruct((half, hidden), jnp.float32),
            jax.ShapeDtypeStruct((half, hidden), jnp.float32),
            jax.ShapeDtypeStruct((1, half), jnp.float32),
        ),
        in_specs=[VMEM] * 4,
        out_specs=(VMEM,) * 3,
        compiler_params=pltpu.CompilerParams(vmem_limit_bytes=12 << 20),
        name="finish",
    )(mine, theirs, w_cut, gain_cut)
    return (in_grad[None], out_grad[None], gain_grad)


def solution(mesh):
    finer = Mesh(
        mesh.devices.reshape(2, 4, 2, mesh.shape["section"]), ("dp_0", "dp_1", "dp_2", "section")
    )
    in_specs = (
        P(DP, None),
        P(DP, None),
        P("section", None, None),
        P("section", None, None),
        P("section", None),
    )
    out_specs = (P("section", DP, None), P("section", DP, None), P("section", DP))
    return jax.shard_map(local, mesh=finer, in_specs=in_specs, out_specs=out_specs, check_vma=False)
```

```python
import functools

import jax
import jax.numpy as jnp
from jax import lax
from jax.experimental import pallas as pl
from jax.experimental.pallas import tpu as pltpu
from jax.sharding import Mesh
from jax.sharding import PartitionSpec as P

ROWS = 16
WAIT = 2
FIRST, SECOND = 4, 8
ROWS_AT = (7, 7, 6, 5)
FIRST_AT = (5, 5, 4, 3)
SECOND_AT = (2, 2, 2, 1)
UNROLL = 8
FLIP = 2
SCOPED = 6 << 20
DP = ("dp_0", "dp_1", "dp_2")
CHIPS = ("dp_0", "dp_1")
CORE = "dp_2"
RING = "dp_1"
FAR = "dp_0"
EPSILON = 1e-05

VMEM = pl.BlockSpec(memory_space=pltpu.VMEM)
SMEM = pl.BlockSpec(memory_space=pltpu.SMEM)
HBM = pl.BlockSpec(memory_space=pltpu.HBM)


def bring_in(low, micro, mine, came_ref, source_ref, rows_ref, sem):
    def fetch():
        copy = pltpu.make_async_copy(source_ref.at[pl.ds(low * ROWS, ROWS), :], rows_ref, sem)
        copy.start()
        copy.wait()

    if came_ref is None:
        fetch()
    elif not 0 <= low < micro:
        rows_ref[...] = came_ref[...]
    else:
        pl.when(mine)(fetch)

        @pl.when(jnp.logical_not(mine))
        def _():
            rows_ref[...] = came_ref[...]


def turned(k, ctl_ref):
    return jnp.bitwise_xor(ctl_ref[ctl_ref.shape[0] - 3], k)


def column_cut(k, size):
    return pl.ds(pl.multiple_of(k * size, size), size)


def forward_body(tick, micro, skipped, flipped, *refs):
    starting = tick == 0
    ctl_ref, source_ref, w_in_far, w_out_far, gain_ref, *refs = refs
    came_ref = None if starting else refs[0]
    (out_ref, rows_all, pre_all, w_in_ref, w_out_ref, rows_ref, source_sem, load_sem) = refs[-8:]
    width, hidden = w_in_ref.shape
    pieces, _, _, size = rows_all.shape
    slot = ctl_ref[tick]

    def load(which, k):
        far, near = ((w_in_far, w_in_ref), (w_out_far, w_out_ref))[which]
        cut = column_cut(k, size)
        return pltpu.make_async_copy(far.at[cut, :], near.at[cut, :], load_sem.at[which, k])

    if starting:
        for which in range(2):
            for k in range(pieces):
                load(which, k).start()
    mine = ctl_ref[ctl_ref.shape[0] - 2] == 1
    bring_in(tick, micro, mine, came_ref, source_ref, rows_ref, source_sem)

    def project(k, carry):
        pre, total = carry
        if starting:
            load(0, k).wait()
        cut = column_cut(k, size)
        rows = rows_ref[:, cut]
        rows_all[turned(k, ctl_ref), slot] = rows
        rows = rows.astype(jnp.float32)
        pre = pre + jnp.dot(
            (rows * gain_ref[:, cut]).astype(jnp.bfloat16), w_in_ref[cut, :], preferred_element_type=jnp.float32
        )
        return pre, total + jnp.sum(rows * rows, axis=1, keepdims=True)

    zeros = jnp.zeros((ROWS, hidden), jnp.float32), jnp.zeros((ROWS, 1), jnp.float32)
    pre, total = lax.fori_loop(0, pieces, project, zeros, unroll=UNROLL)
    row_scale = lax.rsqrt(total / width + EPSILON)
    pre = pre * row_scale
    pre_all[slot, :, :hidden] = pre
    pre_all[slot, :, hidden:] = jnp.broadcast_to(row_scale, (ROWS, 128))
    act = (pre * jax.nn.sigmoid(pre)).astype(jnp.bfloat16)
    if skipped:
        return

    def expand(k, carry):
        if starting:
            load(1, k).wait()
        cut = column_cut(k, size)
        if flipped:
            branch = jnp.dot(act, w_out_ref[:, cut], preferred_element_type=jnp.float32)
        else:
            branch = lax.dot_general(
                act, w_out_ref[cut, :], (((1,), (1,)), ((), ())), preferred_element_type=jnp.float32
            )
        out_ref[:, cut] = (rows_ref[:, cut].astype(jnp.float32) + branch).astype(jnp.bfloat16)
        return carry

    lax.fori_loop(0, pieces, expand, 0, unroll=UNROLL)


def forward_step(tick, micro, skipped, flipped, pieces, ctl, source, w_in, w_out, gain, came, stores):
    width, hidden = w_in.shape
    starting = tick == 0
    weight = HBM if starting else VMEM
    return pl.pallas_call(
        functools.partial(forward_body, tick, micro, skipped, flipped),
        out_shape=(
            jax.ShapeDtypeStruct((ROWS, width), jnp.bfloat16),
            pltpu.VMEM((pieces, micro + 1, ROWS, width // pieces), jnp.bfloat16),
            pltpu.VMEM((micro + 1, ROWS, hidden + 128), jnp.float32),
            pltpu.VMEM(w_in.shape, jnp.bfloat16),
            pltpu.VMEM(w_out.shape, jnp.bfloat16),
        ),
        in_specs=[SMEM, HBM, weight, weight, VMEM] + [VMEM] * (0 if starting else 3),
        out_specs=(VMEM,) * 5,
        scratch_shapes=[
            pltpu.VMEM((ROWS, width), jnp.bfloat16),
            pltpu.SemaphoreType.DMA,
            pltpu.SemaphoreType.DMA((2, pieces)),
        ],
        input_output_aliases={} if starting else {2: 3, 3: 4, 6: 1, 7: 2},
        compiler_params=pltpu.CompilerParams(vmem_limit_bytes=SCOPED),
        name="forward_step",
    )(ctl, source, w_in, w_out, gain, *(() if starting else (came, *stores)))


def flip_body(far_ref, near_ref, flat_ref):
    for low in range(0, far_ref.shape[0], 512):
        flat_ref[:, low : low + 512] = jnp.transpose(near_ref[low : low + 512, :])


def flip(weight):
    return pl.pallas_call(
        flip_body,
        out_shape=(pltpu.VMEM(weight.shape, weight.dtype), pltpu.VMEM(weight.shape[::-1], weight.dtype)),
        in_specs=[VMEM],
        out_specs=(VMEM, VMEM),
        input_output_aliases={0: 0},
        cost_estimate=pl.CostEstimate(flops=5_000_000_000, transcendentals=0, bytes_accessed=16_000_000),
        compiler_params=pltpu.CompilerParams(vmem_limit_bytes=SCOPED),
        name="flip",
    )(weight)


def backward_body(tick, micro, last, *refs):
    ends = micro + 2 * last - 1
    starting = tick == last
    ctl_ref, source_ref, w_in_in, w_out_in, gain_ref, rows_in, pre_in, *refs = refs
    came_ref = None if starting else refs[0]
    (out_ref, rows_all, pre_all, up_all, pair_all, w_in_ref, w_out_ref, up_ref, sem) = refs[-9:]
    width, hidden = w_out_ref.shape
    pieces, _, _, size = rows_all.shape
    slot = ctl_ref[micro + tick]
    mine = ctl_ref[ctl_ref.shape[0] - 1] == 1
    bring_in(tick - last, micro, mine, came_ref, source_ref, up_ref, sem)

    def project(k, total):
        cut = column_cut(k, size)
        up = up_ref[:, cut]
        up_all[turned(k, ctl_ref), slot] = up
        return total + jnp.dot(up, w_out_ref[cut, :], preferred_element_type=jnp.float32)

    grad_act = lax.fori_loop(0, pieces, project, jnp.zeros((ROWS, hidden), jnp.float32), unroll=UNROLL)
    pre = pre_all[slot, :, :hidden]
    row_scale = pre_all[slot, :, hidden : hidden + 1]
    sig = jax.nn.sigmoid(pre)
    grad_pre = grad_act * sig * (1.0 + pre * (1.0 - sig))
    scaled = (grad_pre * row_scale).astype(jnp.bfloat16)
    pair_all[slot, :, :hidden] = scaled
    pair_all[slot, :, hidden:] = (pre * sig).astype(jnp.bfloat16)
    if tick == ends:
        return
    pull = jnp.sum(scaled.astype(jnp.float32) * pre, axis=1, keepdims=True) * row_scale / width

    def expand(k, carry):
        cut = column_cut(k, size)
        grad_norm = jnp.dot(scaled, w_in_ref[:, cut], preferred_element_type=jnp.float32)
        out_ref[:, cut] = (
            up_ref[:, cut].astype(jnp.float32)
            + grad_norm * gain_ref[:, cut]
            - rows_all[turned(k, ctl_ref), slot].astype(jnp.float32) * pull
        ).astype(jnp.bfloat16)
        return carry

    lax.fori_loop(0, pieces, expand, 0, unroll=UNROLL)


def backward_step(tick, micro, last, pieces, ctl, source, w_in, w_out, gain, stores, came, kept):
    width, hidden = w_out.shape
    starting = tick == last
    size = width // pieces
    return pl.pallas_call(
        functools.partial(backward_body, tick, micro, last),
        out_shape=(
            jax.ShapeDtypeStruct((ROWS, width), jnp.bfloat16),
            pltpu.VMEM((pieces, micro + 1, ROWS, size), jnp.bfloat16),
            pltpu.VMEM((micro + 1, ROWS, hidden + 128), jnp.float32),
            pltpu.VMEM((pieces, micro + 1, ROWS, size), jnp.bfloat16),
            pltpu.VMEM((micro + 1, ROWS, 2 * hidden), jnp.bfloat16),
            pltpu.VMEM(w_in.shape, jnp.bfloat16),
            pltpu.VMEM(w_out.shape, jnp.bfloat16),
        ),
        in_specs=[SMEM, HBM] + [VMEM] * (5 if starting else 8),
        out_specs=(VMEM,) * 7,
        scratch_shapes=[pltpu.VMEM((ROWS, width), jnp.bfloat16), pltpu.SemaphoreType.DMA],
        input_output_aliases={2: 5, 3: 6, 5: 1, 6: 2, **({} if starting else {8: 3, 9: 4})},
        compiler_params=pltpu.CompilerParams(vmem_limit_bytes=SCOPED),
        name="backward_step",
    )(ctl, source, w_in, w_out, gain, *stores, *(() if starting else (came, *kept)))


def gradient_body(plan, ctl_ref, *refs):
    count = 1 + max(entry[0] for entry in plan)
    sources, refs = refs[:count], refs[count:]
    mine_in, theirs_in, mine_out, theirs_out, rows_buf, up_buf, pair_buf, sems = refs
    bufs = (rows_buf.at[0], rows_buf.at[1], up_buf.at[0], up_buf.at[1], pair_buf)
    copies = [
        pltpu.make_async_copy(sources[k].at[pl.ds(low, size), :], bufs[which].at[pl.ds(at, size), :], sems.at[n])
        for n, (k, low, size, which, at) in enumerate(plan)
    ]
    for copy in copies:
        copy.start()
    for copy in copies:
        copy.wait()
    hidden = pair_buf.shape[1] // 2
    half = rows_buf.shape[2] // 2
    core = ctl_ref[ctl_ref.shape[0] - 4]
    for buf, right, outs in (
        (rows_buf, pair_buf[:, :hidden], (mine_in, theirs_in)),
        (up_buf, pair_buf[:, hidden:], (mine_out, theirs_out)),
    ):
        for which, out_ref in enumerate(outs):
            low = pl.multiple_of((core if which == 0 else 1 - core) * half, half)
            for tile in range(2):
                value = lax.dot_general(
                    buf[tile, :, pl.ds(low, half)],
                    right,
                    (((0,), (0,)), ((), ())),
                    preferred_element_type=jnp.float32,
                )
                out_ref[tile] = value.astype(out_ref.dtype)


def gradient_step(ctl, groups, sent, micro):
    plan, sources = [], []
    for name, content in groups.items():
        for d, piece in enumerate(sent[name]):
            base = 0
            for kind, first, stop in content:
                for tile in range(1 if kind == 2 else 2):
                    size = (stop - first) * ROWS
                    plan.append((len(sources) + d, base, size, 2 * kind + tile, (d * micro + first) * ROWS))
                    base += size
        sources += sent[name]
    size = sources[0].shape[1]
    tokens = micro * ROWS * len(sent[name])
    pairs = (2, size // 2, size // 2)
    return pl.pallas_call(
        functools.partial(gradient_body, tuple(plan)),
        out_shape=(
            jax.ShapeDtypeStruct(pairs, jnp.float32),
            jax.ShapeDtypeStruct(pairs, jnp.bfloat16),
        )
        * 2,
        in_specs=[SMEM] + [pl.BlockSpec(memory_space=pl.ANY)] * len(sources),
        out_specs=(VMEM,) * 4,
        scratch_shapes=[
            pltpu.VMEM((2, tokens, size), jnp.bfloat16),
            pltpu.VMEM((2, tokens, size), jnp.bfloat16),
            pltpu.VMEM((tokens, size), jnp.bfloat16),
            pltpu.SemaphoreType.DMA((len(plan),)),
        ],
        compiler_params=pltpu.CompilerParams(vmem_limit_bytes=20 << 20),
        name="gradient_step",
    )(ctl, *sources)


def finish_body(mine_ref, near_ref, far_ref, w_ref, gain_ref, in_ref, sum_ref):
    hidden = in_ref.shape[1]
    plain = mine_ref[0] + near_ref[0].astype(jnp.float32) + far_ref[...].astype(jnp.float32)
    in_ref[...] = plain * gain_ref[:, :1]
    ones = jnp.ones((8, hidden), jnp.float32)
    sum_ref[...] = lax.dot_general(
        ones,
        plain * w_ref[...].astype(jnp.float32),
        (((1,), (1,)), ((), ())),
        precision=lax.Precision.HIGHEST,
        preferred_element_type=jnp.float32,
    )[:1]


def local(inputs, cotangent, weight_in, weight_out, norm_gains):
    gain = norm_gains
    tokens, width = inputs.shape
    hidden = weight_in.shape[2]
    micro = tokens // ROWS
    sections = lax.axis_size("section")
    last = sections - 1
    pos = lax.axis_index("section")
    chips = lax.axis_size(CHIPS)
    half = width // (chips * lax.axis_size(CORE))
    size = width // chips
    onward = [(i, (i + 1) % sections) for i in range(sections)]
    back = [((i + 1) % sections, i) for i in range(sections)]
    ticks = jnp.arange(micro + last)
    which = jnp.concatenate([ticks - pos, ticks - last + pos])
    slots = jnp.where((which >= 0) & (which < micro), which, micro)
    own = jnp.stack([lax.axis_index(CORE), lax.axis_index(CHIPS), pos == 0, pos == last])
    ctl = jnp.concatenate([slots, own]).astype(jnp.int32)
    low = lax.axis_index(DP) * half
    gain_cut = jnp.broadcast_to(lax.dynamic_slice_in_dim(gain[0], low, half, 0)[:, None], (half, 128))
    w_cut = lax.dynamic_slice_in_dim(weight_in[0], low, half, 0)
    ctl, gain_cut, w_cut, inputs, cotangent, w_in_near, w_out_near = lax.optimization_barrier(
        (ctl, gain_cut, w_cut, inputs, cotangent, weight_in[0], weight_out[0])
    )
    inputs, cotangent, w_in_near, w_out_near = (
        pltpu.with_memory_space_constraint(array, pltpu.HBM)
        for array in (inputs, cotangent, w_in_near, w_out_near)
    )

    rings = lax.axis_size(RING)

    def shift(tile, d):
        return lax.ppermute(tile, RING, [(i, i ^ d) for i in range(rings)]) if d else tile

    groups = {
        "rows": ((0, 0, micro),),
        "first": ((1, 0, FIRST), (2, 0, FIRST)),
        "second": ((1, FIRST, SECOND), (2, FIRST, SECOND)),
        "third": ((1, SECOND, micro), (2, SECOND, micro)),
    }
    sent = {name: [None] * rings for name in groups}
    leaving = {}
    end = micro + 2 * last - 1
    for name, when in (
        ("rows", ROWS_AT),
        ("first", FIRST_AT),
        ("second", SECOND_AT),
        ("third", (0,) * rings),
    ):
        for d, back_by in enumerate(when):
            leaving.setdefault(end - back_by, []).append((name, d))

    stores = kept = came = arriving = None
    for tick in range(micro + 2 * last):
        if tick < micro + last:
            flipped = tick >= FLIP
            out = w_out_flat if flipped else w_out_near
            made, *stores, w_in_near, out = forward_step(
                tick, micro, tick == micro + last - 1, flipped, chips, ctl, inputs, w_in_near, out, gain, came, stores
            )
            if flipped:
                w_out_flat = out
            else:
                w_out_near = out
            came = lax.ppermute(made, "section", onward)
            if tick == FLIP - 2:
                w_out_near, w_out_flat = flip(w_out_near)
            if tick == FLIP - 1:
                w_in_near, w_in_flat = flip(w_in_near)
        due = leaving.get(tick - WAIT, ()) if tick >= last else ()
        if due:
            arriving, *pieces = lax.optimization_barrier((arriving, *(sent[name][d] for name, d in due)))
            for (name, d), piece in zip(due, pieces):
                sent[name][d] = piece
        if tick >= last:
            made, *both, w_in_flat, w_out_near = backward_step(
                tick, micro, last, chips, ctl, cotangent, w_in_flat, w_out_near, gain, stores, arriving, kept
            )
            stores, kept = both[:2], both[2:]
            if tick < end:
                arriving = lax.ppermute(made, "section", back)
            for name, d in leaving.get(tick, ()):
                tiles = []
                for kind, low, high in groups[name]:
                    if kind == 2:
                        tiles.append(kept[1][low:high])
                    else:
                        store = kept[0] if kind else stores[0]
                        tiles += [store[d, low:high], store[d + rings, low:high]]
                tiles = [tile.reshape(-1, size) for tile in tiles]
                sent[name][d] = shift(jnp.concatenate(tiles), d)
    sums = gradient_step(ctl, groups, sent, micro)
    parts = []
    for mine, theirs in (sums[:2], sums[2:]):
        near = lax.ppermute(theirs, CORE, [(0, 1), (1, 0)])
        far = (mine[1] + near[1].astype(jnp.float32)).astype(jnp.bfloat16)
        parts.append((mine, near, lax.ppermute(far, FAR, [(0, 1), (1, 0)])))
    in_grad, gain_grad = pl.pallas_call(
        finish_body,
        out_shape=(
            jax.ShapeDtypeStruct((half, hidden), jnp.float32),
            jax.ShapeDtypeStruct((1, half), jnp.float32),
        ),
        in_specs=[VMEM] * 5,
        out_specs=(VMEM,) * 2,
        compiler_params=pltpu.CompilerParams(vmem_limit_bytes=12 << 20),
        name="finish",
    )(*parts[0], w_cut, gain_cut)
    mine, near, far = parts[1]
    out_grad = mine[0] + near[0].astype(jnp.float32) + far.astype(jnp.float32)
    return (in_grad[None], out_grad[None], gain_grad)


def solution(mesh):
    finer = Mesh(
        mesh.devices.reshape(2, 4, 2, mesh.shape["section"]), ("dp_0", "dp_1", "dp_2", "section")
    )
    in_specs = (
        P(DP, None),
        P(DP, None),
        P("section", None, None),
        P("section", None, None),
        P("section", None),
    )
    out_specs = (P("section", DP, None), P("section", DP, None), P("section", DP))
    return jax.shard_map(local, mesh=finer, in_specs=in_specs, out_specs=out_specs, check_vma=False)
```

```python
import functools

import jax
import jax.numpy as jnp
from jax import lax
from jax.experimental import pallas as pl
from jax.experimental.pallas import tpu as pltpu
from jax.sharding import Mesh
from jax.sharding import PartitionSpec as P

ROWS = 16
WAIT = 2
FIRST, SECOND = 4, 8
ROWS_AT = (7, 7, 6, 5)
FIRST_AT = (5, 5, 4, 3)
SECOND_AT = (2, 2, 2, 1)
UNROLL = 8
FLIP = 2
SCOPED = 6 << 20
DP = ("dp_0", "dp_1", "dp_2")
CHIPS = ("dp_0", "dp_1")
CORE = "dp_2"
RING = "dp_1"
FAR = "dp_0"
EPSILON = 1e-05

VMEM = pl.BlockSpec(memory_space=pltpu.VMEM)
SMEM = pl.BlockSpec(memory_space=pltpu.SMEM)
HBM = pl.BlockSpec(memory_space=pltpu.HBM)


def bring_in(low, micro, mine, came_ref, source_ref, rows_ref, sem):
    def fetch():
        copy = pltpu.make_async_copy(source_ref.at[pl.ds(low * ROWS, ROWS), :], rows_ref, sem)
        copy.start()
        copy.wait()

    if came_ref is None:
        fetch()
    elif not 0 <= low < micro:
        rows_ref[...] = came_ref[...]
    else:
        pl.when(mine)(fetch)

        @pl.when(jnp.logical_not(mine))
        def _():
            rows_ref[...] = came_ref[...]


def turned(k, ctl_ref):
    return jnp.bitwise_xor(ctl_ref[ctl_ref.shape[0] - 3], k)


def column_cut(k, size):
    return pl.ds(pl.multiple_of(k * size, size), size)


def forward_body(tick, micro, skipped, flipped, *refs):
    starting = tick == 0
    ctl_ref, source_ref, w_in_far, w_out_far, gain_ref, *refs = refs
    came_ref = None if starting else refs[0]
    (out_ref, rows_all, pre_all, w_in_ref, w_out_ref, rows_ref, source_sem, load_sem) = refs[-8:]
    width, hidden = w_in_ref.shape
    pieces, _, _, size = rows_all.shape
    slot = ctl_ref[tick]

    def load(which, k):
        far, near = ((w_in_far, w_in_ref), (w_out_far, w_out_ref))[which]
        cut = column_cut(k, size)
        return pltpu.make_async_copy(far.at[cut, :], near.at[cut, :], load_sem.at[which, k])

    if starting:
        for which in range(2):
            for k in range(pieces):
                load(which, k).start()
    mine = ctl_ref[ctl_ref.shape[0] - 2] == 1
    bring_in(tick, micro, mine, came_ref, source_ref, rows_ref, source_sem)

    def project(k, carry):
        pre, total = carry
        if starting:
            load(0, k).wait()
        cut = column_cut(k, size)
        rows = rows_ref[:, cut]
        rows_all[turned(k, ctl_ref), slot] = rows
        rows = rows.astype(jnp.float32)
        pre = pre + jnp.dot(
            (rows * gain_ref[:, cut]).astype(jnp.bfloat16), w_in_ref[cut, :], preferred_element_type=jnp.float32
        )
        return pre, total + jnp.sum(rows * rows, axis=1, keepdims=True)

    zeros = jnp.zeros((ROWS, hidden), jnp.float32), jnp.zeros((ROWS, 1), jnp.float32)
    pre, total = lax.fori_loop(0, pieces, project, zeros, unroll=UNROLL)
    row_scale = lax.rsqrt(total / width + EPSILON)
    pre = pre * row_scale
    pre_all[slot, :, :hidden] = pre
    pre_all[slot, :, hidden:] = jnp.broadcast_to(row_scale, (ROWS, 128))
    act = (pre * jax.nn.sigmoid(pre)).astype(jnp.bfloat16)
    if skipped:
        return

    def expand(k, carry):
        if starting:
            load(1, k).wait()
        cut = column_cut(k, size)
        if flipped:
            branch = jnp.dot(act, w_out_ref[:, cut], preferred_element_type=jnp.float32)
        else:
            branch = lax.dot_general(
                act, w_out_ref[cut, :], (((1,), (1,)), ((), ())), preferred_element_type=jnp.float32
            )
        out_ref[:, cut] = (rows_ref[:, cut].astype(jnp.float32) + branch).astype(jnp.bfloat16)
        return carry

    lax.fori_loop(0, pieces, expand, 0, unroll=UNROLL)


def forward_step(tick, micro, skipped, flipped, pieces, ctl, source, w_in, w_out, gain, came, stores):
    width, hidden = w_in.shape
    starting = tick == 0
    weight = HBM if starting else VMEM
    return pl.pallas_call(
        functools.partial(forward_body, tick, micro, skipped, flipped),
        out_shape=(
            jax.ShapeDtypeStruct((ROWS, width), jnp.bfloat16),
            pltpu.VMEM((pieces, micro + 1, ROWS, width // pieces), jnp.bfloat16),
            pltpu.VMEM((micro + 1, ROWS, hidden + 128), jnp.float32),
            pltpu.VMEM(w_in.shape, jnp.bfloat16),
            pltpu.VMEM(w_out.shape, jnp.bfloat16),
        ),
        in_specs=[SMEM, HBM, weight, weight, VMEM] + [VMEM] * (0 if starting else 3),
        out_specs=(VMEM,) * 5,
        scratch_shapes=[
            pltpu.VMEM((ROWS, width), jnp.bfloat16),
            pltpu.SemaphoreType.DMA,
            pltpu.SemaphoreType.DMA((2, pieces)),
        ],
        input_output_aliases={} if starting else {2: 3, 3: 4, 6: 1, 7: 2},
        compiler_params=pltpu.CompilerParams(vmem_limit_bytes=SCOPED),
        name="forward_step",
    )(ctl, source, w_in, w_out, gain, *(() if starting else (came, *stores)))


def flip_body(far_ref, near_ref, flat_ref):
    for low in range(0, far_ref.shape[0], 512):
        flat_ref[:, low : low + 512] = jnp.transpose(near_ref[low : low + 512, :])


def flip(weight):
    return pl.pallas_call(
        flip_body,
        out_shape=(pltpu.VMEM(weight.shape, weight.dtype), pltpu.VMEM(weight.shape[::-1], weight.dtype)),
        in_specs=[VMEM],
        out_specs=(VMEM, VMEM),
        input_output_aliases={0: 0},
        cost_estimate=pl.CostEstimate(flops=5_000_000_000, transcendentals=0, bytes_accessed=16_000_000),
        compiler_params=pltpu.CompilerParams(vmem_limit_bytes=SCOPED),
        name="flip",
    )(weight)


def backward_body(tick, micro, last, *refs):
    ends = micro + 2 * last - 1
    starting = tick == last
    ctl_ref, source_ref, w_in_in, w_out_in, gain_ref, rows_in, pre_in, *refs = refs
    came_ref = None if starting else refs[0]
    (out_ref, rows_all, pre_all, up_all, pair_all, w_in_ref, w_out_ref, up_ref, sem) = refs[-9:]
    width, hidden = w_out_ref.shape
    pieces, _, _, size = rows_all.shape
    slot = ctl_ref[micro + tick]
    mine = ctl_ref[ctl_ref.shape[0] - 1] == 1
    bring_in(tick - last, micro, mine, came_ref, source_ref, up_ref, sem)

    def project(k, total):
        cut = column_cut(k, size)
        up = up_ref[:, cut]
        up_all[turned(k, ctl_ref), slot] = up
        return total + jnp.dot(up, w_out_ref[cut, :], preferred_element_type=jnp.float32)

    grad_act = lax.fori_loop(0, pieces, project, jnp.zeros((ROWS, hidden), jnp.float32), unroll=UNROLL)
    pre = pre_all[slot, :, :hidden]
    row_scale = pre_all[slot, :, hidden : hidden + 1]
    sig = jax.nn.sigmoid(pre)
    grad_pre = grad_act * sig * (1.0 + pre * (1.0 - sig))
    scaled = (grad_pre * row_scale).astype(jnp.bfloat16)
    pair_all[slot, :, :hidden] = scaled
    pair_all[slot, :, hidden:] = (pre * sig).astype(jnp.bfloat16)
    if tick == ends:
        return
    pull = jnp.sum(scaled.astype(jnp.float32) * pre, axis=1, keepdims=True) * row_scale / width

    def expand(k, carry):
        cut = column_cut(k, size)
        grad_norm = jnp.dot(scaled, w_in_ref[:, cut], preferred_element_type=jnp.float32)
        out_ref[:, cut] = (
            up_ref[:, cut].astype(jnp.float32)
            + grad_norm * gain_ref[:, cut]
            - rows_all[turned(k, ctl_ref), slot].astype(jnp.float32) * pull
        ).astype(jnp.bfloat16)
        return carry

    lax.fori_loop(0, pieces, expand, 0, unroll=UNROLL)


def backward_step(tick, micro, last, pieces, ctl, source, w_in, w_out, gain, stores, came, kept):
    width, hidden = w_out.shape
    starting = tick == last
    size = width // pieces
    return pl.pallas_call(
        functools.partial(backward_body, tick, micro, last),
        out_shape=(
            jax.ShapeDtypeStruct((ROWS, width), jnp.bfloat16),
            pltpu.VMEM((pieces, micro + 1, ROWS, size), jnp.bfloat16),
            pltpu.VMEM((micro + 1, ROWS, hidden + 128), jnp.float32),
            pltpu.VMEM((pieces, micro + 1, ROWS, size), jnp.bfloat16),
            pltpu.VMEM((micro + 1, ROWS, 2 * hidden), jnp.bfloat16),
            pltpu.VMEM(w_in.shape, jnp.bfloat16),
            pltpu.VMEM(w_out.shape, jnp.bfloat16),
        ),
        in_specs=[SMEM, HBM] + [VMEM] * (5 if starting else 8),
        out_specs=(VMEM,) * 7,
        scratch_shapes=[pltpu.VMEM((ROWS, width), jnp.bfloat16), pltpu.SemaphoreType.DMA],
        input_output_aliases={2: 5, 3: 6, 5: 1, 6: 2, **({} if starting else {8: 3, 9: 4})},
        compiler_params=pltpu.CompilerParams(vmem_limit_bytes=SCOPED),
        name="backward_step",
    )(ctl, source, w_in, w_out, gain, *stores, *(() if starting else (came, *kept)))


def gradient_body(plan, adding, ctl_ref, *refs):
    count = 1 + max(entry[0] for entry in plan)
    sources, refs = refs[:count], refs[count:]
    *before, rows_buf, up_buf, pair_buf, sems = refs
    outs = before[2 if adding else 0 :]
    bufs = (rows_buf.at[0], rows_buf.at[1], up_buf.at[0], up_buf.at[1], pair_buf)
    copies = [
        pltpu.make_async_copy(sources[k].at[pl.ds(low, size), :], bufs[which].at[pl.ds(at, size), :], sems.at[n])
        for n, (k, low, size, which, at) in enumerate(plan)
    ]
    for copy in copies:
        copy.start()
    for copy in copies:
        copy.wait()
    hidden = pair_buf.shape[1] // 2
    half = rows_buf.shape[2] // 2
    core = ctl_ref[ctl_ref.shape[0] - 4]
    for side, buf in enumerate((rows_buf, up_buf)):
        right = pair_buf[:, side * hidden : (side + 1) * hidden]
        for which in range(2):
            low = pl.multiple_of((core if which == 0 else 1 - core) * half, half) if adding else which * half
            for tile in range(2):
                value = lax.dot_general(
                    buf[tile, :, pl.ds(low, half)],
                    right,
                    (((0,), (0,)), ((), ())),
                    preferred_element_type=jnp.float32,
                )
                if adding:
                    value = value + before[side][tile, pl.ds(low, half), :]
                    out_ref = outs[2 * side + which]
                    out_ref[tile] = value.astype(out_ref.dtype)
                else:
                    outs[side][tile, pl.ds(low, half), :] = value


def gradient_step(ctl, groups, sent, span, before):
    low, high = span
    plan, sources = [], []
    for name, content in groups.items():
        if all(stop <= low or first >= high for _, first, stop in content):
            continue
        for d, piece in enumerate(sent[name]):
            base = 0
            for kind, first, stop in content:
                for tile in range(1 if kind == 2 else 2):
                    start, end = max(first, low), min(stop, high)
                    at = (d * (high - low) + start - low) * ROWS
                    plan.append(
                        (len(sources) + d, base + (start - first) * ROWS, (end - start) * ROWS, 2 * kind + tile, at)
                    )
                    base += (stop - first) * ROWS
        sources += sent[name]
    size = sources[0].shape[1]
    tokens = (high - low) * ROWS * len(sent[name])
    adding = before is not None
    pairs = (2, size // 2, size // 2)
    if adding:
        out_shape = (jax.ShapeDtypeStruct(pairs, jnp.float32), jax.ShapeDtypeStruct(pairs, jnp.bfloat16)) * 2
    else:
        out_shape = (jax.ShapeDtypeStruct((2, size, size // 2), jnp.float32),) * 2
    return pl.pallas_call(
        functools.partial(gradient_body, tuple(plan), adding),
        out_shape=out_shape,
        in_specs=[SMEM] + [pl.BlockSpec(memory_space=pl.ANY)] * len(sources) + [VMEM] * (2 if adding else 0),
        out_specs=(VMEM,) * len(out_shape),
        scratch_shapes=[
            pltpu.VMEM((2, tokens, size), jnp.bfloat16),
            pltpu.VMEM((2, tokens, size), jnp.bfloat16),
            pltpu.VMEM((tokens, size), jnp.bfloat16),
            pltpu.SemaphoreType.DMA((len(plan),)),
        ],
        compiler_params=pltpu.CompilerParams(vmem_limit_bytes=20 << 20),
        name="gradient_step",
    )(ctl, *sources, *(before or ()))


def finish_body(mine_ref, near_ref, far_ref, w_ref, gain_ref, in_ref, sum_ref):
    hidden = in_ref.shape[1]
    plain = mine_ref[0] + near_ref[0].astype(jnp.float32) + far_ref[...].astype(jnp.float32)
    in_ref[...] = plain * gain_ref[:, :1]
    ones = jnp.ones((8, hidden), jnp.float32)
    sum_ref[...] = lax.dot_general(
        ones,
        plain * w_ref[...].astype(jnp.float32),
        (((1,), (1,)), ((), ())),
        precision=lax.Precision.HIGHEST,
        preferred_element_type=jnp.float32,
    )[:1]


def local(inputs, cotangent, weight_in, weight_out, norm_gains):
    gain = norm_gains
    tokens, width = inputs.shape
    hidden = weight_in.shape[2]
    micro = tokens // ROWS
    sections = lax.axis_size("section")
    last = sections - 1
    pos = lax.axis_index("section")
    chips = lax.axis_size(CHIPS)
    half = width // (chips * lax.axis_size(CORE))
    size = width // chips
    onward = [(i, (i + 1) % sections) for i in range(sections)]
    back = [((i + 1) % sections, i) for i in range(sections)]
    ticks = jnp.arange(micro + last)
    which = jnp.concatenate([ticks - pos, ticks - last + pos])
    slots = jnp.where((which >= 0) & (which < micro), which, micro)
    own = jnp.stack([lax.axis_index(CORE), lax.axis_index(CHIPS), pos == 0, pos == last])
    ctl = jnp.concatenate([slots, own]).astype(jnp.int32)
    low = lax.axis_index(DP) * half
    gain_cut = jnp.broadcast_to(lax.dynamic_slice_in_dim(gain[0], low, half, 0)[:, None], (half, 128))
    w_cut = lax.dynamic_slice_in_dim(weight_in[0], low, half, 0)
    ctl, gain_cut, w_cut, inputs, cotangent, w_in_near, w_out_near = lax.optimization_barrier(
        (ctl, gain_cut, w_cut, inputs, cotangent, weight_in[0], weight_out[0])
    )
    inputs, cotangent, w_in_near, w_out_near = (
        pltpu.with_memory_space_constraint(array, pltpu.HBM)
        for array in (inputs, cotangent, w_in_near, w_out_near)
    )

    rings = lax.axis_size(RING)

    def shift(tile, d):
        return lax.ppermute(tile, RING, [(i, i ^ d) for i in range(rings)]) if d else tile

    groups = {
        "rows": ((0, 0, micro),),
        "first": ((1, 0, FIRST), (2, 0, FIRST)),
        "second": ((1, FIRST, SECOND), (2, FIRST, SECOND)),
        "third": ((1, SECOND, micro), (2, SECOND, micro)),
    }
    sent = {name: [None] * rings for name in groups}
    leaving = {}
    end = micro + 2 * last - 1
    for name, when in (
        ("rows", ROWS_AT),
        ("first", FIRST_AT),
        ("second", SECOND_AT),
        ("third", (0,) * rings),
    ):
        for d, back_by in enumerate(when):
            leaving.setdefault(end - back_by, []).append((name, d))

    stores = kept = came = arriving = None
    for tick in range(micro + 2 * last):
        if tick < micro + last:
            flipped = tick >= FLIP
            out = w_out_flat if flipped else w_out_near
            made, *stores, w_in_near, out = forward_step(
                tick, micro, tick == micro + last - 1, flipped, chips, ctl, inputs, w_in_near, out, gain, came, stores
            )
            if flipped:
                w_out_flat = out
            else:
                w_out_near = out
            came = lax.ppermute(made, "section", onward)
            if tick == FLIP - 2:
                w_out_near, w_out_flat = flip(w_out_near)
            if tick == FLIP - 1:
                w_in_near, w_in_flat = flip(w_in_near)
        due = leaving.get(tick - WAIT, ()) if tick >= last else ()
        if due:
            arriving, *pieces = lax.optimization_barrier((arriving, *(sent[name][d] for name, d in due)))
            for (name, d), piece in zip(due, pieces):
                sent[name][d] = piece
        if tick >= last:
            made, *both, w_in_flat, w_out_near = backward_step(
                tick, micro, last, chips, ctl, cotangent, w_in_flat, w_out_near, gain, stores, arriving, kept
            )
            stores, kept = both[:2], both[2:]
            if tick < end:
                arriving = lax.ppermute(made, "section", back)
            for name, d in leaving.get(tick, ()):
                tiles = []
                for kind, low, high in groups[name]:
                    if kind == 2:
                        tiles.append(kept[1][low:high])
                    else:
                        store = kept[0] if kind else stores[0]
                        tiles += [store[d, low:high], store[d + rings, low:high]]
                tiles = [tile.reshape(-1, size) for tile in tiles]
                sent[name][d] = shift(jnp.concatenate(tiles), d)
    before = gradient_step(ctl, groups, sent, (0, SECOND), None)
    sums = gradient_step(ctl, groups, sent, (SECOND, micro), before)
    parts = []
    for mine, theirs in (sums[:2], sums[2:]):
        near = lax.ppermute(theirs, CORE, [(0, 1), (1, 0)])
        far = (mine[1] + near[1].astype(jnp.float32)).astype(jnp.bfloat16)
        parts.append((mine, near, lax.ppermute(far, FAR, [(0, 1), (1, 0)])))
    in_grad, gain_grad = pl.pallas_call(
        finish_body,
        out_shape=(
            jax.ShapeDtypeStruct((half, hidden), jnp.float32),
            jax.ShapeDtypeStruct((1, half), jnp.float32),
        ),
        in_specs=[VMEM] * 5,
        out_specs=(VMEM,) * 2,
        compiler_params=pltpu.CompilerParams(vmem_limit_bytes=12 << 20),
        name="finish",
    )(*parts[0], w_cut, gain_cut)
    mine, near, far = parts[1]
    out_grad = mine[0] + near[0].astype(jnp.float32) + far.astype(jnp.float32)
    return (in_grad[None], out_grad[None], gain_grad)


def solution(mesh):
    finer = Mesh(
        mesh.devices.reshape(2, 4, 2, mesh.shape["section"]), ("dp_0", "dp_1", "dp_2", "section")
    )
    in_specs = (
        P(DP, None),
        P(DP, None),
        P("section", None, None),
        P("section", None, None),
        P("section", None),
    )
    out_specs = (P("section", DP, None), P("section", DP, None), P("section", DP))
    return jax.shard_map(local, mesh=finer, in_specs=in_specs, out_specs=out_specs, check_vma=False)
```

```python
import functools

import jax
import jax.numpy as jnp
from jax import lax
from jax.experimental import pallas as pl
from jax.experimental.pallas import tpu as pltpu
from jax.sharding import Mesh
from jax.sharding import PartitionSpec as P

ROWS = 16
WAIT = 2
FIRST, SECOND = 4, 8
ROWS_AT = (7, 7, 6, 5)
FIRST_AT = (5, 5, 4, 3)
SECOND_AT = (2, 2, 2, 1)
UNROLL = 8
FLIP = 2
SCOPED = 6 << 20
DP = ("dp_0", "dp_1", "dp_2")
CHIPS = ("dp_0", "dp_1")
CORE = "dp_2"
RING = "dp_1"
FAR = "dp_0"
EPSILON = 1e-05

VMEM = pl.BlockSpec(memory_space=pltpu.VMEM)
SMEM = pl.BlockSpec(memory_space=pltpu.SMEM)
HBM = pl.BlockSpec(memory_space=pltpu.HBM)


def bring_in(low, micro, mine, came_ref, source_ref, rows_ref, sem):
    def fetch():
        copy = pltpu.make_async_copy(source_ref.at[pl.ds(low * ROWS, ROWS), :], rows_ref, sem)
        copy.start()
        copy.wait()

    if came_ref is None:
        fetch()
    elif not 0 <= low < micro:
        rows_ref[...] = came_ref[...]
    else:
        pl.when(mine)(fetch)

        @pl.when(jnp.logical_not(mine))
        def _():
            rows_ref[...] = came_ref[...]


def turned(k, ctl_ref):
    return jnp.bitwise_xor(ctl_ref[ctl_ref.shape[0] - 3], k)


def column_cut(k, size):
    return pl.ds(pl.multiple_of(k * size, size), size)


def forward_body(tick, micro, skipped, flipped, *refs):
    starting = tick == 0
    ctl_ref, source_ref, w_in_far, w_out_far, gain_ref, *refs = refs
    came_ref = None if starting else refs[0]
    (out_ref, rows_all, pre_all, w_in_ref, w_out_ref, rows_ref, source_sem, load_sem) = refs[-8:]
    width, hidden = w_in_ref.shape
    pieces, _, _, size = rows_all.shape
    slot = ctl_ref[tick]

    def load(which, k):
        far, near = ((w_in_far, w_in_ref), (w_out_far, w_out_ref))[which]
        cut = column_cut(k, size)
        return pltpu.make_async_copy(far.at[cut, :], near.at[cut, :], load_sem.at[which, k])

    if starting:
        for which in range(2):
            for k in range(pieces):
                load(which, k).start()
    mine = ctl_ref[ctl_ref.shape[0] - 2] == 1
    bring_in(tick, micro, mine, came_ref, source_ref, rows_ref, source_sem)

    def project(k, carry):
        pre, total = carry
        if starting:
            load(0, k).wait()
        cut = column_cut(k, size)
        rows = rows_ref[:, cut]
        rows_all[turned(k, ctl_ref), slot] = rows
        rows = rows.astype(jnp.float32)
        pre = pre + jnp.dot(
            (rows * gain_ref[:, cut]).astype(jnp.bfloat16), w_in_ref[cut, :], preferred_element_type=jnp.float32
        )
        return pre, total + jnp.sum(rows * rows, axis=1, keepdims=True)

    zeros = jnp.zeros((ROWS, hidden), jnp.float32), jnp.zeros((ROWS, 1), jnp.float32)
    pre, total = lax.fori_loop(0, pieces, project, zeros, unroll=UNROLL)
    row_scale = lax.rsqrt(total / width + EPSILON)
    pre = pre * row_scale
    pre_all[slot, :, :hidden] = pre
    pre_all[slot, :, hidden:] = jnp.broadcast_to(row_scale, (ROWS, 128))
    act = (pre * jax.nn.sigmoid(pre)).astype(jnp.bfloat16)
    if skipped:
        return

    def expand(k, carry):
        if starting:
            load(1, k).wait()
        cut = column_cut(k, size)
        if flipped:
            branch = jnp.dot(act, w_out_ref[:, cut], preferred_element_type=jnp.float32)
        else:
            branch = lax.dot_general(
                act, w_out_ref[cut, :], (((1,), (1,)), ((), ())), preferred_element_type=jnp.float32
            )
        out_ref[:, cut] = (rows_ref[:, cut].astype(jnp.float32) + branch).astype(jnp.bfloat16)
        return carry

    lax.fori_loop(0, pieces, expand, 0, unroll=UNROLL)


def forward_step(tick, micro, skipped, flipped, pieces, ctl, source, w_in, w_out, gain, came, stores):
    width, hidden = w_in.shape
    starting = tick == 0
    weight = HBM if starting else VMEM
    return pl.pallas_call(
        functools.partial(forward_body, tick, micro, skipped, flipped),
        out_shape=(
            jax.ShapeDtypeStruct((ROWS, width), jnp.bfloat16),
            pltpu.VMEM((pieces, micro + 1, ROWS, width // pieces), jnp.bfloat16),
            pltpu.VMEM((micro + 1, ROWS, hidden + 128), jnp.float32),
            pltpu.VMEM(w_in.shape, jnp.bfloat16),
            pltpu.VMEM(w_out.shape, jnp.bfloat16),
        ),
        in_specs=[SMEM, HBM, weight, weight, VMEM] + [VMEM] * (0 if starting else 3),
        out_specs=(VMEM,) * 5,
        scratch_shapes=[
            pltpu.VMEM((ROWS, width), jnp.bfloat16),
            pltpu.SemaphoreType.DMA,
            pltpu.SemaphoreType.DMA((2, pieces)),
        ],
        input_output_aliases={} if starting else {2: 3, 3: 4, 6: 1, 7: 2},
        compiler_params=pltpu.CompilerParams(vmem_limit_bytes=SCOPED),
        name="forward_step",
    )(ctl, source, w_in, w_out, gain, *(() if starting else (came, *stores)))


def flip_body(far_ref, near_ref, flat_ref):
    for low in range(0, far_ref.shape[0], 512):
        flat_ref[:, low : low + 512] = jnp.transpose(near_ref[low : low + 512, :])


def flip(weight):
    return pl.pallas_call(
        flip_body,
        out_shape=(pltpu.VMEM(weight.shape, weight.dtype), pltpu.VMEM(weight.shape[::-1], weight.dtype)),
        in_specs=[VMEM],
        out_specs=(VMEM, VMEM),
        input_output_aliases={0: 0},
        cost_estimate=pl.CostEstimate(flops=5_000_000_000, transcendentals=0, bytes_accessed=16_000_000),
        compiler_params=pltpu.CompilerParams(vmem_limit_bytes=SCOPED),
        name="flip",
    )(weight)


def backward_body(tick, micro, last, *refs):
    ends = micro + 2 * last - 1
    starting = tick == last
    ctl_ref, source_ref, w_in_in, w_out_in, gain_ref, rows_in, pre_in, *refs = refs
    came_ref = None if starting else refs[0]
    (out_ref, rows_all, pre_all, up_all, pair_all, w_in_ref, w_out_ref, up_ref, sem) = refs[-9:]
    width, hidden = w_out_ref.shape
    pieces, _, _, size = rows_all.shape
    slot = ctl_ref[micro + tick]
    mine = ctl_ref[ctl_ref.shape[0] - 1] == 1
    bring_in(tick - last, micro, mine, came_ref, source_ref, up_ref, sem)

    def project(k, total):
        cut = column_cut(k, size)
        up = up_ref[:, cut]
        up_all[turned(k, ctl_ref), slot] = up
        return total + jnp.dot(up, w_out_ref[cut, :], preferred_element_type=jnp.float32)

    grad_act = lax.fori_loop(0, pieces, project, jnp.zeros((ROWS, hidden), jnp.float32), unroll=UNROLL)
    pre = pre_all[slot, :, :hidden]
    row_scale = pre_all[slot, :, hidden : hidden + 1]
    sig = jax.nn.sigmoid(pre)
    grad_pre = grad_act * sig * (1.0 + pre * (1.0 - sig))
    scaled = (grad_pre * row_scale).astype(jnp.bfloat16)
    pair_all[slot, :, :hidden] = scaled
    pair_all[slot, :, hidden:] = (pre * sig).astype(jnp.bfloat16)
    if tick == ends:
        return
    pull = jnp.sum(scaled.astype(jnp.float32) * pre, axis=1, keepdims=True) * row_scale / width

    def expand(k, carry):
        cut = column_cut(k, size)
        grad_norm = jnp.dot(scaled, w_in_ref[:, cut], preferred_element_type=jnp.float32)
        out_ref[:, cut] = (
            up_ref[:, cut].astype(jnp.float32)
            + grad_norm * gain_ref[:, cut]
            - rows_all[turned(k, ctl_ref), slot].astype(jnp.float32) * pull
        ).astype(jnp.bfloat16)
        return carry

    lax.fori_loop(0, pieces, expand, 0, unroll=UNROLL)


def backward_step(tick, micro, last, pieces, ctl, source, w_in, w_out, gain, stores, came, kept):
    width, hidden = w_out.shape
    starting = tick == last
    size = width // pieces
    return pl.pallas_call(
        functools.partial(backward_body, tick, micro, last),
        out_shape=(
            jax.ShapeDtypeStruct((ROWS, width), jnp.bfloat16),
            pltpu.VMEM((pieces, micro + 1, ROWS, size), jnp.bfloat16),
            pltpu.VMEM((micro + 1, ROWS, hidden + 128), jnp.float32),
            pltpu.VMEM((pieces, micro + 1, ROWS, size), jnp.bfloat16),
            pltpu.VMEM((micro + 1, ROWS, 2 * hidden), jnp.bfloat16),
            pltpu.VMEM(w_in.shape, jnp.bfloat16),
            pltpu.VMEM(w_out.shape, jnp.bfloat16),
        ),
        in_specs=[SMEM, HBM] + [VMEM] * (5 if starting else 8),
        out_specs=(VMEM,) * 7,
        scratch_shapes=[pltpu.VMEM((ROWS, width), jnp.bfloat16), pltpu.SemaphoreType.DMA],
        input_output_aliases={2: 5, 3: 6, 5: 1, 6: 2, **({} if starting else {8: 3, 9: 4})},
        compiler_params=pltpu.CompilerParams(vmem_limit_bytes=SCOPED),
        name="backward_step",
    )(ctl, source, w_in, w_out, gain, *stores, *(() if starting else (came, *kept)))


def gradient_body(plan, adding, ctl_ref, *refs):
    count = 1 + max(entry[0] for entry in plan)
    sources, refs = refs[:count], refs[count:]
    *before, rows_buf, up_buf, pair_buf, sems = refs
    outs = before[2 if adding else 0 :]
    bufs = (rows_buf.at[0], rows_buf.at[1], up_buf.at[0], up_buf.at[1], pair_buf)
    copies = [
        pltpu.make_async_copy(sources[k].at[pl.ds(low, size), :], bufs[which].at[pl.ds(at, size), :], sems.at[n])
        for n, (k, low, size, which, at) in enumerate(plan)
    ]
    for copy in copies:
        copy.start()
    for copy in copies:
        copy.wait()
    hidden = pair_buf.shape[1] // 2
    half = rows_buf.shape[2] // 2
    core = ctl_ref[ctl_ref.shape[0] - 4]
    for side, buf in enumerate((rows_buf, up_buf)):
        right = pair_buf[:, side * hidden : (side + 1) * hidden]
        for which in range(2):
            low = pl.multiple_of((core if which == 0 else 1 - core) * half, half) if adding else which * half
            for tile in range(2):
                value = lax.dot_general(
                    buf[tile, :, pl.ds(low, half)],
                    right,
                    (((0,), (0,)), ((), ())),
                    preferred_element_type=jnp.float32,
                )
                if adding:
                    value = value + before[side][tile, pl.ds(low, half), :]
                    out_ref = outs[2 * side + which]
                    out_ref[tile] = value.astype(out_ref.dtype)
                else:
                    outs[side][tile, pl.ds(low, half), :] = value


def gradient_step(ctl, groups, sent, span, before):
    low, high = span
    plan, sources = [], []
    for name, content in groups.items():
        if all(stop <= low or first >= high for _, first, stop in content):
            continue
        for d, piece in enumerate(sent[name]):
            base = 0
            for kind, first, stop in content:
                for tile in range(1 if kind == 2 else 2):
                    start, end = max(first, low), min(stop, high)
                    at = (d * (high - low) + start - low) * ROWS
                    plan.append(
                        (len(sources) + d, base + (start - first) * ROWS, (end - start) * ROWS, 2 * kind + tile, at)
                    )
                    base += (stop - first) * ROWS
        sources += sent[name]
    size = sources[0].shape[1]
    tokens = (high - low) * ROWS * len(sent[name])
    adding = before is not None
    pairs = (2, size // 2, size // 2)
    if adding:
        out_shape = (jax.ShapeDtypeStruct(pairs, jnp.float32), jax.ShapeDtypeStruct(pairs, jnp.bfloat16)) * 2
    else:
        out_shape = (jax.ShapeDtypeStruct((2, size, size // 2), jnp.float32),) * 2
    return pl.pallas_call(
        functools.partial(gradient_body, tuple(plan), adding),
        out_shape=out_shape,
        in_specs=[SMEM] + [pl.BlockSpec(memory_space=pl.ANY)] * len(sources) + [VMEM] * (2 if adding else 0),
        out_specs=(VMEM,) * len(out_shape),
        scratch_shapes=[
            pltpu.VMEM((2, tokens, size), jnp.bfloat16),
            pltpu.VMEM((2, tokens, size), jnp.bfloat16),
            pltpu.VMEM((tokens, size), jnp.bfloat16),
            pltpu.SemaphoreType.DMA((len(plan),)),
        ],
        compiler_params=pltpu.CompilerParams(vmem_limit_bytes=20 << 20),
        name="gradient_step",
    )(ctl, *sources, *(before or ()))


def finish_body(mine_ref, near_ref, far_ref, w_ref, gain_ref, in_ref, sum_ref):
    hidden = in_ref.shape[1]
    plain = mine_ref[0] + near_ref[0].astype(jnp.float32) + far_ref[...].astype(jnp.float32)
    in_ref[...] = plain * gain_ref[:, :1]
    ones = jnp.ones((8, hidden), jnp.float32)
    sum_ref[...] = lax.dot_general(
        ones,
        plain * w_ref[...].astype(jnp.float32),
        (((1,), (1,)), ((), ())),
        precision=lax.Precision.HIGHEST,
        preferred_element_type=jnp.float32,
    )[:1]


def local(inputs, cotangent, weight_in, weight_out, norm_gains):
    gain = norm_gains
    tokens, width = inputs.shape
    hidden = weight_in.shape[2]
    micro = tokens // ROWS
    sections = lax.axis_size("section")
    last = sections - 1
    pos = lax.axis_index("section")
    chips = lax.axis_size(CHIPS)
    half = width // (chips * lax.axis_size(CORE))
    size = width // chips
    onward = [(i, (i + 1) % sections) for i in range(sections)]
    back = [((i + 1) % sections, i) for i in range(sections)]
    ticks = jnp.arange(micro + last)
    which = jnp.concatenate([ticks - pos, ticks - last + pos])
    slots = jnp.where((which >= 0) & (which < micro), which, micro)
    own = jnp.stack([lax.axis_index(CORE), lax.axis_index(CHIPS), pos == 0, pos == last])
    ctl = jnp.concatenate([slots, own]).astype(jnp.int32)
    own_low = lax.axis_index(DP) * half
    ctl, own_low, inputs, cotangent, w_in_near, w_out_near = lax.optimization_barrier(
        (ctl, own_low, inputs, cotangent, weight_in[0], weight_out[0])
    )
    inputs, cotangent, w_in_near, w_out_near = (
        pltpu.with_memory_space_constraint(array, pltpu.HBM)
        for array in (inputs, cotangent, w_in_near, w_out_near)
    )

    rings = lax.axis_size(RING)

    def shift(tile, d):
        return lax.ppermute(tile, RING, [(i, i ^ d) for i in range(rings)]) if d else tile

    groups = {
        "rows": ((0, 0, micro),),
        "first": ((1, 0, FIRST), (2, 0, FIRST)),
        "second": ((1, FIRST, SECOND), (2, FIRST, SECOND)),
        "third": ((1, SECOND, micro), (2, SECOND, micro)),
    }
    sent = {name: [None] * rings for name in groups}
    leaving = {}
    end = micro + 2 * last - 1
    for name, when in (
        ("rows", ROWS_AT),
        ("first", FIRST_AT),
        ("second", SECOND_AT),
        ("third", (0,) * rings),
    ):
        for d, back_by in enumerate(when):
            leaving.setdefault(end - back_by, []).append((name, d))

    stores = kept = came = arriving = None
    for tick in range(micro + 2 * last):
        if tick < micro + last:
            flipped = tick >= FLIP
            out = w_out_flat if flipped else w_out_near
            made, *stores, w_in_near, out = forward_step(
                tick, micro, tick == micro + last - 1, flipped, chips, ctl, inputs, w_in_near, out, gain, came, stores
            )
            if flipped:
                w_out_flat = out
            else:
                w_out_near = out
            came = lax.ppermute(made, "section", onward)
            if tick == FLIP - 2:
                w_out_near, w_out_flat = flip(w_out_near)
            if tick == FLIP - 1:
                w_in_near, w_in_flat = flip(w_in_near)
        due = leaving.get(tick - WAIT, ()) if tick >= last else ()
        if due:
            arriving, *pieces = lax.optimization_barrier((arriving, *(sent[name][d] for name, d in due)))
            for (name, d), piece in zip(due, pieces):
                sent[name][d] = piece
        if tick >= last:
            made, *both, w_in_flat, w_out_near = backward_step(
                tick, micro, last, chips, ctl, cotangent, w_in_flat, w_out_near, gain, stores, arriving, kept
            )
            stores, kept = both[:2], both[2:]
            if tick < end:
                arriving = lax.ppermute(made, "section", back)
            for name, d in leaving.get(tick, ()):
                tiles = []
                for kind, low, high in groups[name]:
                    if kind == 2:
                        tiles.append(kept[1][low:high])
                    else:
                        store = kept[0] if kind else stores[0]
                        tiles += [store[d, low:high], store[d + rings, low:high]]
                tiles = [tile.reshape(-1, size) for tile in tiles]
                sent[name][d] = shift(jnp.concatenate(tiles), d)
    before = gradient_step(ctl, groups, sent, (0, SECOND), None)
    sums = gradient_step(ctl, groups, sent, (SECOND, micro), before)
    parts = []
    for mine, theirs in (sums[:2], sums[2:]):
        near = lax.ppermute(theirs, CORE, [(0, 1), (1, 0)])
        far = (mine[1] + near[1].astype(jnp.float32)).astype(jnp.bfloat16)
        parts.append((mine, near, lax.ppermute(far, FAR, [(0, 1), (1, 0)])))
    late_gain, late_w, _ = lax.optimization_barrier((gain, weight_in[0], sums[1]))
    gain_cut = jnp.broadcast_to(lax.dynamic_slice_in_dim(late_gain[0], own_low, half, 0)[:, None], (half, 128))
    w_cut = lax.dynamic_slice_in_dim(late_w, own_low, half, 0)
    in_grad, gain_grad = pl.pallas_call(
        finish_body,
        out_shape=(
            jax.ShapeDtypeStruct((half, hidden), jnp.float32),
            jax.ShapeDtypeStruct((1, half), jnp.float32),
        ),
        in_specs=[VMEM] * 5,
        out_specs=(VMEM,) * 2,
        compiler_params=pltpu.CompilerParams(vmem_limit_bytes=12 << 20),
        name="finish",
    )(*parts[0], w_cut, gain_cut)
    mine, near, far = parts[1]
    out_grad = mine[0] + near[0].astype(jnp.float32) + far.astype(jnp.float32)
    return (in_grad[None], out_grad[None], gain_grad)


def solution(mesh):
    finer = Mesh(
        mesh.devices.reshape(2, 4, 2, mesh.shape["section"]), ("dp_0", "dp_1", "dp_2", "section")
    )
    in_specs = (
        P(DP, None),
        P(DP, None),
        P("section", None, None),
        P("section", None, None),
        P("section", None),
    )
    out_specs = (P("section", DP, None), P("section", DP, None), P("section", DP))
    return jax.shard_map(local, mesh=finer, in_specs=in_specs, out_specs=out_specs, check_vma=False)
```
